32 devices in a mesh: dp: 4 (over y, x), seq: 8 (over z, core).
Axes of the slice: x: 2, y: 2, z: 4, core: 2. Of those that a mesh axis runs over, the one named last changes fastest.
Arguments:
- inputs: bfloat16 [8, 1024, 1024], P('dp', 'seq'), may hold values from -6 to 6
- cotangent: bfloat16 [8, 1024, 1024], P('dp', 'seq'), may hold values from -6 to 6
- lengths: int32 [8], P('dp'), may hold values from 256 to 1024, as said below
- block_order: int32 [16], replicated, may hold values from 0 to 15, each once
- step_count: int32 [], replicated, may hold values from 2 to 20
- learn_rates: float32 [6], replicated, as said below
- w_qkv: float32 [1024, 3072], P(('dp', 'seq')), may hold values from -0.1875 to 0.1875
- w_proj: float32 [1024, 1024], P(('dp', 'seq')), may hold values from -1.5 to 1.5
- w_expand: float32 [1024, 4096], P(('dp', 'seq')), may hold values from -0.1875 to 0.1875
- w_shrink: float32 [4096, 1024], P(('dp', 'seq')), may hold values from -0.09375 to 0.09375
- vectors: float32 [1024, 8], P(('dp', 'seq')), as said below
- bias_expand: float32 [4096], P(('dp', 'seq')), may hold values from -1 to 1
- first_qkv: float32 [1024, 3072], P(('dp', 'seq')), may hold values from -0.00018310547 to 0.00018310547
- first_proj: float32 [1024, 1024], P(('dp', 'seq')), may hold values from -0.00018310547 to 0.00018310547
- first_expand: float32 [1024, 4096], P(('dp', 'seq')), may hold values from -0.00018310547 to 0.00018310547
- first_shrink: float32 [4096, 1024], P(('dp', 'seq')), may hold values from -0.00018310547 to 0.00018310547
- first_vectors: float32 [1024, 8], P(('dp', 'seq')), may hold values from -0.00018310547 to 0.00018310547
- first_bias: float32 [4096], P(('dp', 'seq')), may hold values from -0.00018310547 to 0.00018310547
- second_qkv: float32 [1024, 3072], P(('dp', 'seq')), may hold values from 4.207952e-09 to 1.6673019e-08
- second_proj: float32 [1024, 1024], P(('dp', 'seq')), may hold values from 4.207952e-09 to 1.6673019e-08
- second_expand: float32 [1024, 4096], P(('dp', 'seq')), may hold values from 4.207952e-09 to 1.6673019e-08
- second_shrink: float32 [4096, 1024], P(('dp', 'seq')), may hold values from 4.207952e-09 to 1.6673019e-08
- second_vectors: float32 [1024, 8], P(('dp', 'seq')), may hold values from 4.207952e-09 to 1.6673019e-08
- second_bias: float32 [4096], P(('dp', 'seq')), may hold values from 4.207952e-09 to 1.6673019e-08
Outputs:
- layer_out: float32 [8, 1024, 1024], P('dp', 'seq')
- grad_inputs: float32 [8, 1024, 1024], P('dp', 'seq')
- grad_norm: float32 [], replicated
- new_qkv: float32 [1024, 3072], P(('dp', 'seq'))
- new_proj: float32 [1024, 1024], P(('dp', 'seq'))
- new_expand: float32 [1024, 4096], P(('dp', 'seq'))
- new_shrink: float32 [4096, 1024], P(('dp', 'seq'))
- new_vectors: float32 [1024, 8], P(('dp', 'seq'))
- new_bias: float32 [4096], P(('dp', 'seq'))
- new_first_qkv: float32 [1024, 3072], P(('dp', 'seq'))
- new_first_proj: float32 [1024, 1024], P(('dp', 'seq'))
- new_first_expand: float32 [1024, 4096], P(('dp', 'seq'))
- new_first_shrink: float32 [4096, 1024], P(('dp', 'seq'))
- new_first_vectors: float32 [1024, 8], P(('dp', 'seq'))
- new_first_bias: float32 [4096], P(('dp', 'seq'))
- new_second_qkv: float32 [1024, 3072], P(('dp', 'seq'))
- new_second_proj: float32 [1024, 1024], P(('dp', 'seq'))
- new_second_expand: float32 [1024, 4096], P(('dp', 'seq'))
- new_second_shrink: float32 [4096, 1024], P(('dp', 'seq'))
- new_second_vectors: float32 [1024, 8], P(('dp', 'seq'))
- new_second_bias: float32 [4096], P(('dp', 'seq'))
The draws below stay inside these ranges and needn't reach their ends.
Inputs may be any that keep to these rules, and one draw needn't show every extreme that they name: `lengths`: slots from a sequence's length on are padding; some sequence is full and some has exactly 256 valid slots. A permutation: block b of 64 slots of every sequence holds positions block_order[b] * 64 onward. `learn_rates`: positive rates in the order w_qkv, w_proj, w_expand, w_shrink, vectors, bias_expand. `vectors`: columns 0 and 5 are gains near one, the other columns biases.
All inputs are finite; a program needn't handle non-finite values.
Results may differ from the reference program's by a relative error of at most 0.009.
The reference program's roundings to bfloat16 on the way count: a program that leaves them out, or rounds other values in their place, can miss the bound.
Values may be sent and summed in bfloat16 or wider, within the bound.
A program may use at most 104 MiB of HBM per device.

```python
import math
import jax
import jax.numpy as jnp
from jax import lax

D = 1024
HEADS = 16
HD = 64
FF = 4096
L = 1024
SEQS = 8
NBLK = 16
NPARAM = 12595200


def draw_lengths(key, part):
    key_one, key_two, key_three = jax.random.split(key, 3)
    drawn = jax.random.randint(key_one, (SEQS,), L // 4, L + 1, dtype=jnp.int32)
    full_at = jax.random.randint(key_two, (), 0, SEQS, dtype=jnp.int32)
    short_at = (full_at + 1 + jax.random.randint(key_three, (), 0, SEQS - 1, dtype=jnp.int32)) % SEQS
    drawn = drawn.at[full_at].set(L)
    drawn = drawn.at[short_at].set(L // 4)
    return drawn


def draw_learn_rates(key, part):
    base_rates = jnp.array([2.0 * D ** (-0.5), 2.0 * (D // 64) ** (-0.5), 2.0 * D ** (-0.5), 2.0 * FF ** (-0.5), 0.2, 0.2], jnp.float32)
    factor = jnp.exp(jax.random.uniform(key, (6,), jnp.float32, math.log(0.5), math.log(2.0)))
    return base_rates * factor


def draw_vectors(key, part):
    key_one, key_two = jax.random.split(key)
    gains = 1.0 + 0.15 * jax.random.uniform(key_one, (D, 8), jnp.float32, -1.0, 1.0)
    biases = jnp.clip(0.2 * jax.random.normal(key_two, (D, 8), jnp.float32), -1.0, 1.0)
    columns = jnp.arange(8)
    is_gain = (columns == 0) | (columns == 5)
    return jnp.where(is_gain[None, :], gains, biases)


def shard_levels(key, shape, cuts, least, high):
    def one(position, blocks):
        steps = jax.random.uniform(jax.random.fold_in(jax.random.fold_in(key, 6), position), (blocks,), jnp.float32, least / len(cuts), high / len(cuts))
        return jnp.repeat(jnp.exp(steps), shape[position] // blocks).reshape((-1,) + (1,) * (len(shape) - position - 1))

    level = one(*cuts[0])
    for cut in cuts[1:]:
        level = level * one(*cut)
    return level


def noise(rng, dims, scale, bound, cuts=(), kind=jnp.bfloat16):
    values = jax.random.normal(rng, dims, jnp.float32) * scale
    if len(cuts) > 0:
        values = shard_levels(rng, dims, cuts, -0.22, 0.18) * values
    return jnp.clip(values, min=-bound, max=bound).astype(kind)


def setup_inputs(seed: int = 0) -> dict:
    arg_keys = jax.random.split(jax.random.key(seed), 25)
    return {
        "inputs": noise(arg_keys[0], (SEQS, L, D), 1.0, 6.0, ((0, 4), (1, 8))),
        "cotangent": noise(arg_keys[1], (SEQS, L, D), 1.0, 6.0, ((0, 4), (1, 8))),
        "lengths": draw_lengths(jax.random.fold_in(arg_keys[24], 71), 0),
        "block_order": jax.random.permutation(arg_keys[3], NBLK).astype(jnp.int32),
        "step_count": jax.random.randint(arg_keys[4], (), 2, 21).astype(jnp.int32),
        "learn_rates": draw_learn_rates(jax.random.fold_in(arg_keys[24], 71), 0),
        "w_qkv": noise(arg_keys[6], (D, 3 * D), D ** -0.5, 0.1875, ((0, 32),), jnp.float32),
        "w_proj": noise(arg_keys[7], (D, D), (D // 64) ** -0.5, 1.5, ((0, 32),), jnp.float32),
        "w_expand": noise(arg_keys[8], (D, FF), D ** -0.5, 0.1875, ((0, 32),), jnp.float32),
        "w_shrink": noise(arg_keys[9], (FF, D), FF ** -0.5, 0.09375, ((0, 32),), jnp.float32),
        "vectors": draw_vectors(jax.random.fold_in(arg_keys[24], 71), 0),
        "bias_expand": noise(arg_keys[11], (FF,), 0.2, 1.0, ((0, 32),), jnp.float32),
        "first_qkv": noise(arg_keys[12], (D, 3 * D), (0.11 * NPARAM ** -0.5), 0.00018310547, ((0, 32),), jnp.float32),
        "first_proj": noise(arg_keys[13], (D, D), (0.11 * NPARAM ** -0.5), 0.00018310547, ((0, 32),), jnp.float32),
        "first_expand": noise(arg_keys[14], (D, FF), (0.11 * NPARAM ** -0.5), 0.00018310547, ((0, 32),), jnp.float32),
        "first_shrink": noise(arg_keys[15], (FF, D), (0.11 * NPARAM ** -0.5), 0.00018310547, ((0, 32),), jnp.float32),
        "first_vectors": noise(arg_keys[16], (D, 8), (0.11 * NPARAM ** -0.5), 0.00018310547, ((0, 32),), jnp.float32),
        "first_bias": noise(arg_keys[17], (FF,), (0.11 * NPARAM ** -0.5), 0.00018310547, ((0, 32),), jnp.float32),
        "second_qkv": jnp.clip(jnp.exp(math.log(1.6673018521373706e-08) - 1.37681564 * jax.random.uniform(arg_keys[18], (D, 3 * D), jnp.float32) ** shard_levels(arg_keys[18], (D, 3 * D), ((0, 32),), -0.2, 0.2)), 4.2079522089011334e-09, 1.6673018521373706e-08),
        "second_proj": jnp.clip(jnp.exp(math.log(1.6673018521373706e-08) - 1.37681564 * jax.random.uniform(arg_keys[19], (D, D), jnp.float32) ** shard_levels(arg_keys[19], (D, D), ((0, 32),), -0.2, 0.2)), 4.2079522089011334e-09, 1.6673018521373706e-08),
        "second_expand": jnp.clip(jnp.exp(math.log(1.6673018521373706e-08) - 1.37681564 * jax.random.uniform(arg_keys[20], (D, FF), jnp.float32) ** shard_levels(arg_keys[20], (D, FF), ((0, 32),), -0.2, 0.2)), 4.2079522089011334e-09, 1.6673018521373706e-08),
        "second_shrink": jnp.clip(jnp.exp(math.log(1.6673018521373706e-08) - 1.37681564 * jax.random.uniform(arg_keys[21], (FF, D), jnp.float32) ** shard_levels(arg_keys[21], (FF, D), ((0, 32),), -0.2, 0.2)), 4.2079522089011334e-09, 1.6673018521373706e-08),
        "second_vectors": jnp.clip(jnp.exp(math.log(1.6673018521373706e-08) - 1.37681564 * jax.random.uniform(arg_keys[22], (D, 8), jnp.float32) ** shard_levels(arg_keys[22], (D, 8), ((0, 32),), -0.2, 0.2)), 4.2079522089011334e-09, 1.6673018521373706e-08),
        "second_bias": jnp.clip(jnp.exp(math.log(1.6673018521373706e-08) - 1.37681564 * jax.random.uniform(arg_keys[23], (FF,), jnp.float32) ** shard_levels(arg_keys[23], (FF,), ((0, 32),), -0.2, 0.2)), 4.2079522089011334e-09, 1.6673018521373706e-08),
    }


@jax.custom_vjp
def low(v):
    return lax.optimization_barrier(v.astype(jnp.bfloat16)).astype(jnp.float32)

@jax.custom_vjp
def low_back(v):
    return v

def low_keep(v):
    return (low(v), None)

def low_pass(kept, grad):
    return (grad,)

def back_keep(v):
    return (v, None)

def back_low(kept, grad):
    return (low(grad),)
low.defvjp(low_keep, low_pass)
low_back.defvjp(back_keep, back_low)
norm_eps = 1e-05
neg_fill = -1e+30
beta_first = 0.9
beta_second = 0.95
adam_eps = 1e-08
decay_rate = 0.1
clip_bound = 1.0

def layer_norm(values, gain_vec, shift_vec):
    centered = values - lax.optimization_barrier(jnp.mean(values, axis=-1, keepdims=True))
    variance = lax.optimization_barrier(jnp.mean(centered * centered, axis=-1, keepdims=True))
    return centered * lax.rsqrt(variance + norm_eps) * gain_vec + shift_vec

def slot_positions(slot_ids, order_table, block_len):
    block_ids = jnp.arange(order_table.shape[0], dtype=jnp.int32)
    one_hot = (slot_ids[:, None] // block_len == block_ids[None, :]).astype(jnp.int32)
    picked = lax.optimization_barrier(jnp.sum(one_hot * order_table[None, :], axis=1)).astype(jnp.int32)
    return picked * block_len + slot_ids % block_len

def matmul(left, right):
    return jnp.dot(left, right, precision=lax.Precision.HIGHEST, preferred_element_type=jnp.float32)

def sequence_forward(params, tokens_seq, length, positions):
    w_qkv, w_proj, w_expand, w_shrink, vectors, bias_expand = params
    qkv_w = low(w_qkv)
    proj_w = low(w_proj)
    expand_w = low(w_expand)
    shrink_w = low(w_shrink)
    vec_low = low(vectors)
    bias_low = low(bias_expand)
    gain_one = vec_low[:, 0]
    shift_one = vec_low[:, 1]
    bias_query = vec_low[:, 2]
    bias_value = vec_low[:, 3]
    bias_proj = vec_low[:, 4]
    gain_two = vec_low[:, 5]
    shift_two = vec_low[:, 6]
    bias_shrink = vec_low[:, 7]
    slot_count = tokens_seq.shape[0]
    score_scale = 1.0 / math.sqrt(HD)
    normed_one = low(layer_norm(tokens_seq, gain_one, shift_one))
    bias_cat = jnp.concatenate([bias_query, jnp.zeros_like(bias_query), bias_value])
    qkv_rows = low_back(low(matmul(normed_one, qkv_w) + bias_cat))
    queries = qkv_rows[:, :D].reshape(slot_count, HEADS, HD)
    key_rows = qkv_rows[:, D:2 * D].reshape(slot_count, HEADS, HD)
    value_rows = qkv_rows[:, 2 * D:].reshape(slot_count, HEADS, HD)
    scores = low_back(jnp.einsum('qhd,khd->hqk', queries, key_rows, precision=lax.Precision.HIGHEST) * score_scale)
    allowed = (positions[None, :] <= positions[:, None]) & (positions[None, :] < length)
    scores = jnp.where(allowed[None], scores, neg_fill)
    row_max = lax.optimization_barrier(jnp.max(scores, axis=-1, keepdims=True))
    exp_scores = jnp.exp(scores - row_max)
    softmax_w = exp_scores / lax.optimization_barrier(jnp.sum(exp_scores, axis=-1, keepdims=True))
    context = jnp.einsum('hqk,khd->qhd', low(softmax_w), value_rows, precision=lax.Precision.HIGHEST)
    context = low_back(low(context.reshape(slot_count, D)))
    attn_out = low_back(matmul(context, proj_w) + bias_proj)
    resid = tokens_seq + attn_out
    normed_two = low(layer_norm(resid, gain_two, shift_two))
    pre_act = low_back(matmul(normed_two, expand_w) + bias_low)
    hidden = low(jax.nn.gelu(pre_act, approximate=True))
    branch = low_back(matmul(hidden, shrink_w) + bias_shrink)
    return resid + branch

def reference(inputs, cotangent, lengths, block_order, step_count, learn_rates, w_qkv, w_proj, w_expand, w_shrink, vectors, bias_expand, first_qkv, first_proj, first_expand, first_shrink, first_vectors, first_bias, second_qkv, second_proj, second_expand, second_shrink, second_vectors, second_bias):
    block_len = L // NBLK
    positions = slot_positions(jnp.arange(L, dtype=jnp.int32), block_order, block_len)
    params = (w_qkv, w_proj, w_expand, w_shrink, vectors, bias_expand)

    def one_sequence(carry, packed):
        tokens_seq, cot_seq, length = packed

        def forward(prm, values):
            return sequence_forward(prm, values, length, positions)
        result, back_fn = jax.vjp(forward, params, tokens_seq.astype(jnp.float32))
        valid_rows = (positions < length).astype(jnp.float32)
        grad_params, grad_tokens = back_fn(cot_seq.astype(jnp.float32) * valid_rows[:, None])
        carry = jax.tree.map(lambda total, extra: total + extra, carry, grad_params)
        return (carry, (result, grad_tokens))
    zero_grads = jax.tree.map(jnp.zeros_like, params)
    grads, (layer_out, grad_inputs) = lax.scan(one_sequence, zero_grads, (inputs, cotangent, lengths))
    square_sum = sum((jnp.sum(gradient * gradient) for gradient in grads))
    grad_norm = jnp.sqrt(square_sum)
    clip_factor = clip_bound / jnp.maximum(grad_norm, clip_bound)
    step_float = step_count.astype(jnp.float32)
    correct_first = 1.0 - beta_first ** step_float
    correct_second = 1.0 - beta_second ** step_float
    firsts = (first_qkv, first_proj, first_expand, first_shrink, first_vectors, first_bias)
    seconds = (second_qkv, second_proj, second_expand, second_shrink, second_vectors, second_bias)
    renewed = []
    first_new = []
    second_new = []
    for group_id in range(6):
        clipped = grads[group_id] * clip_factor
        moment_one = beta_first * firsts[group_id] + (1.0 - beta_first) * clipped
        moment_two = beta_second * seconds[group_id] + (1.0 - beta_second) * clipped * clipped
        update = moment_one / correct_first / (jnp.sqrt(moment_two / correct_second) + adam_eps)
        if group_id < 4:
            update = update + decay_rate * params[group_id]
        renewed.append(params[group_id] - learn_rates[group_id] * update)
        first_new.append(moment_one)
        second_new.append(moment_two)
    return (layer_out, grad_inputs, grad_norm, renewed[0], renewed[1], renewed[2], renewed[3], renewed[4], renewed[5], first_new[0], first_new[1], first_new[2], first_new[3], first_new[4], first_new[5], second_new[0], second_new[1], second_new[2], second_new[3], second_new[4], second_new[5])
```

```python
import functools
import math

import jax
import jax.numpy as jnp
from jax import lax
from jax.experimental import pallas as pl
from jax.experimental.pallas import tpu as pltpu
from jax.sharding import PartitionSpec as P

HEADS = 16
HD = 64
MESH = pl.DeviceIdType.MESH


norm_eps = 1e-05
neg_fill = -1e30
beta_first = 0.9
beta_second = 0.95
adam_eps = 1e-08
decay_rate = 0.1
clip_bound = 1.0


def flip(index, mask):
    return index + mask * (1 - 2 * ((index // mask) % 2))


class Place:
    def __init__(self, dp_size, seq_size):
        self.dp_size = dp_size
        self.depth = seq_size // 2
        self.bits = dp_size.bit_length() - 1
        self.dp = lax.axis_index("dp")
        seq = lax.axis_index("seq")
        self.z = seq // 2
        self.core = seq % 2
        self.masks = self.masks_of(self.core)

    def masks_of(self, core):
        return [
            (1 - core) * 2 ** (k % self.bits) + core * 2 ** ((k + 1) % self.bits)
            for k in range(self.bits)
        ]

    def leaving(self, core_masks=None):
        masks = self.masks if core_masks is None else core_masks
        order = []
        for k in range(self.bits - 1, -1, -1):
            order = order + self.span(flip(self.dp, masks[k]), k, masks)
        return order + [self.dp]

    def cube(self, k):
        return (flip(self.dp, self.masks[k]), self.z * 2 + self.core)

    def span(self, start, k, masks=None):
        found = [start]
        for mask in (self.masks if masks is None else masks)[:k]:
            found = found + [flip(one, mask) for one in found]
        return found

    def sibling(self):
        return (self.dp, self.z * 2 + 1 - self.core)

    def line(self, j):
        return (self.dp, ((self.z + j) % self.depth) * 2 + self.core)


def greet(peers):
    barrier = pltpu.get_barrier_semaphore()
    for peer in peers:
        pl.semaphore_signal(barrier, inc=1, device_id=peer, device_id_type=MESH)
    pl.semaphore_wait(barrier, len(peers))


def gather_kernel(dp_size, seq_size, count, *refs):
    sources, fulls = refs[:count], refs[count : 2 * count]
    local_sem, line_send, cube_send, pair_send, arrive = refs[2 * count :]
    at = Place(dp_size, seq_size)
    depth, bits, dp, z, core = at.depth, at.bits, at.dp, at.z, at.core
    greet(
        [at.line(j) for j in range(1, depth)] + [at.cube(k) for k in range(bits)] + [at.sibling()]
    )
    pending = []

    def send(a, source, row, level, peer, sem):
        copy = pltpu.make_async_remote_copy(
            src_ref=source,
            dst_ref=fulls[a].at[row, level, core],
            send_sem=sem,
            recv_sem=arrive.at[a, row, level, core],
            device_id=peer,
            device_id_type=MESH,
        )
        copy.start()
        pending.append(copy)

    def received(a, row, level, side):
        block = fulls[a].at[row, level, side]
        pltpu.make_async_copy(block, block, arrive.at[a, row, level, side]).wait()

    def pass_on(a, source, row, slot, level, first):
        for k in range(first, bits):
            send(a, source, row, level, at.cube(k), cube_send.at[a, k, slot, level])
        send(a, source, row, level, at.sibling(), pair_send.at[a, slot, level])

    for a in range(count):
        for j in range(1, depth):
            send(a, sources[a], dp, z, at.line(j), line_send.at[a, j - 1])
        pass_on(a, sources[a], dp, 0, z, 0)
    locals_ = []
    for a in range(count):
        copy = pltpu.make_async_copy(sources[a], fulls[a].at[dp, z, core], local_sem.at[a])
        copy.start()
        locals_.append(copy)

    def line_stage(a):
        for j in range(depth - 1, 0, -1):
            level = (z + j) % depth
            received(a, dp, level, core)
            pass_on(a, fulls[a].at[dp, level, core], dp, 0, level, 0)

    def cube_stage(a, k):
        for slot, row in enumerate(at.span(flip(dp, at.masks[k]), k)):
            for j in range(depth):
                level = (z + j) % depth
                received(a, row, level, core)
                pass_on(a, fulls[a].at[row, level, core], row, 2**k + slot, level, k + 1)

    stages = bits + 1
    for step in range(count + stages - 1):
        for stage in range(stages):
            a = step - stage
            if 0 <= a < count:
                if stage == 0:
                    line_stage(a)
                else:
                    cube_stage(a, stage - 1)
    for a in range(count):
        for row in range(dp_size):
            for level in range(depth):
                received(a, row, level, 1 - core)
    for copy in locals_:
        copy.wait()
    for copy in pending:
        copy.wait_send()


def gather_all(blocks, dp_size, seq_size):
    count = len(blocks)
    depth, bits = seq_size // 2, dp_size.bit_length() - 1
    shapes = [
        jax.ShapeDtypeStruct((dp_size, depth, 2) + block.shape, block.dtype) for block in blocks
    ]
    return pl.pallas_call(
        functools.partial(gather_kernel, dp_size, seq_size, count),
        out_shape=shapes,
        in_specs=[pl.BlockSpec(memory_space=pl.ANY)] * count,
        out_specs=[pl.BlockSpec(memory_space=pl.ANY)] * count,
        scratch_shapes=[
            pltpu.SemaphoreType.DMA((count,)),
            pltpu.SemaphoreType.DMA((count, depth - 1)),
            pltpu.SemaphoreType.DMA((count, bits, dp_size, depth)),
            pltpu.SemaphoreType.DMA((count, dp_size, depth)),
            pltpu.SemaphoreType.DMA((count, dp_size, depth, 2)),
        ],
        compiler_params=pltpu.CompilerParams(collective_id=0, has_side_effects=True),
        name="gather_all",
    )(*blocks)


def scatter_kernel(dp_size, seq_size, count, *refs):
    at = Place(dp_size, seq_size)
    depth, bits, dp, z, core = at.depth, at.bits, at.dp, at.z, at.core
    grads, outs, norm_out = refs[:count], refs[count : 2 * count], refs[2 * count]
    scratch = refs[2 * count + 1 :]
    own, pair = scratch[:count], scratch[count : 2 * count]
    cube = [scratch[(2 + k) * count : (3 + k) * count] for k in range(bits)]
    line = scratch[(2 + bits) * count : (3 + bits) * count]
    seq_part, dp_part, mine = scratch[(3 + bits) * count : (3 + bits) * count + 3]
    (own_sem, pair_send, pair_recv, cube_send, cube_recv, line_send, line_recv) = scratch[
        (3 + bits) * count + 3 : (3 + bits) * count + 10
    ]
    norm_send, norm_recv = scratch[(3 + bits) * count + 10 :]
    seq = z * 2 + core
    seq_peers = [(dp, (seq + j) % seq_size) for j in range(1, seq_size)]
    dp_peers = [((dp + j) % dp_size, seq) for j in range(1, dp_size)]
    greet(seq_peers + dp_peers)
    pending = []

    order = at.leaving()
    theirs = at.leaving(at.masks_of(1 - core))
    for a in range(count):
        for spot, row in enumerate(order):
            copy = pltpu.make_async_remote_copy(
                src_ref=grads[a].at[theirs[spot], :, 1 - core],
                dst_ref=pair[a].at[theirs[spot]],
                send_sem=pair_send.at[a, spot],
                recv_sem=pair_recv.at[a, theirs[spot]],
                device_id=at.sibling(),
                device_id_type=MESH,
            )
            copy.start()
            pending.append(copy)
            pltpu.make_async_copy(
                grads[a].at[row, :, core], own[a].at[row], own_sem.at[a, spot]
            ).start()

    def ready(a, spot):
        row = order[spot]
        pltpu.make_async_copy(grads[a].at[row, :, core], own[a].at[row], own_sem.at[a, spot]).wait()
        pltpu.make_async_copy(pair[a].at[row], pair[a].at[row], pair_recv.at[a, row]).wait()

    def total(a, row, level, rows, hops):
        value = own[a][row, level, rows].astype(jnp.float32)
        value = value + pair[a][row, level, rows].astype(jnp.float32)
        for k, slot in hops:
            value = value + cube[k][a][slot, level, rows].astype(jnp.float32)
        return value

    def each_chunk(a, body):
        height = own[a].shape[2]
        step = min(16, height)
        if step == height:
            body(pl.ds(0, step))
        else:

            def one(i, carry):
                body(pl.ds(pl.multiple_of(i * step, step), step))
                return carry

            lax.fori_loop(0, height // step, one, 0)

    def fold(a, row, hops):
        for level in range(depth):

            def body(rows, level=level):
                own[a][row, level, rows] = total(a, row, level, rows, hops).astype(own[a].dtype)

            each_chunk(a, body)

    def cube_stage(a, k):
        leave = at.span(flip(dp, at.masks[k]), k)
        for slot, row in enumerate(leave):
            spot = spot_of(bits, k, slot)
            ready(a, spot)
            landed = [(q, landing_slot(bits, k, slot, q)) for q in range(k + 1, bits)]
            for q, hop_slot in landed:
                block = cube[q][a].at[hop_slot]
                pltpu.make_async_copy(block, block, cube_recv.at[a, q, hop_slot]).wait()
            fold(a, row, landed)
            copy = pltpu.make_async_remote_copy(
                src_ref=own[a].at[row],
                dst_ref=cube[k][a].at[slot],
                send_sem=cube_send.at[a, k, slot],
                recv_sem=cube_recv.at[a, k, slot],
                device_id=at.cube(k),
                device_id_type=MESH,
            )
            copy.start()
            pending.append(copy)

    all_hops = [(q, 0) for q in range(bits)]

    def line_stage(a):
        ready(a, len(order) - 1)
        for q, hop_slot in all_hops:
            block = cube[q][a].at[hop_slot]
            pltpu.make_async_copy(block, block, cube_recv.at[a, q, hop_slot]).wait()
        for j in range(1, depth):
            level = (z + j) % depth

            def body(rows, level=level):
                own[a][dp, level, rows] = total(a, dp, level, rows, all_hops).astype(own[a].dtype)

            each_chunk(a, body)
            copy = pltpu.make_async_remote_copy(
                src_ref=own[a].at[dp, level],
                dst_ref=line[a].at[j - 1],
                send_sem=line_send.at[a, j - 1],
                recv_sem=line_recv.at[a, j - 1],
                device_id=at.line(j),
                device_id_type=MESH,
            )
            copy.start()
            pending.append(copy)

    mine[...] = jnp.zeros_like(mine)

    def final_stage(a):
        for j in range(1, depth):
            block = line[a].at[j - 1]
            pltpu.make_async_copy(block, block, line_recv.at[a, j - 1]).wait()

        def body(rows):
            value = total(a, dp, z, rows, all_hops)
            for j in range(1, depth):
                value = value + line[a][j - 1, rows].astype(jnp.float32)
            outs[a][rows] = value
            squares = value * value
            height, width = squares.shape
            folded = squares.reshape(height // 8, 8, width).sum(0)
            part = folded[:, :128]
            for lane in range(1, width // 128):
                part = part + folded[:, lane * 128 : (lane + 1) * 128]
            mine[...] += part

        each_chunk(a, body)

    stages = bits + 2
    for step in range(count + stages - 1):
        for stage in range(stages):
            a = step - stage
            if 0 <= a < count:
                if stage < bits:
                    cube_stage(a, bits - 1 - stage)
                elif stage == bits:
                    line_stage(a)
                else:
                    final_stage(a)

    def exchange(peers, parts, base):
        copies = []
        for i, peer in enumerate(peers):
            copy = pltpu.make_async_remote_copy(
                src_ref=mine,
                dst_ref=parts.at[i],
                send_sem=norm_send.at[base + i],
                recv_sem=norm_recv.at[base + i],
                device_id=peer,
                device_id_type=MESH,
            )
            copy.start()
            copies.append(copy)
        for copy in copies:
            copy.wait()

    exchange(seq_peers, seq_part, 0)
    value = mine[...]
    for i in range(seq_size - 1):
        value = value + seq_part[i]
    mine[...] = value
    exchange(dp_peers, dp_part, seq_size - 1)
    value = mine[...]
    for i in range(dp_size - 1):
        value = value + dp_part[i]
    norm_out[...] = value
    for copy in pending:
        copy.wait_send()


def spot_of(bits, k, slot):
    return sum(2**q for q in range(k + 1, bits)) + slot


def landing_slot(bits, k, slot, q):
    return 2**k + slot


def scatter_all(grads, dp_size, seq_size):
    count = len(grads)
    depth, bits = seq_size // 2, dp_size.bit_length() - 1
    tails = [grad.shape[3:] for grad in grads]
    kinds = [grad.dtype for grad in grads]
    scratch = []
    for lead in [(dp_size, depth)] * 2 + [(2**k, depth) for k in range(bits)] + [(depth - 1,)]:
        scratch += [pltpu.VMEM(lead + tail, kind) for tail, kind in zip(tails, kinds)]
    scratch += [
        pltpu.VMEM((seq_size - 1, 8, 128), jnp.float32),
        pltpu.VMEM((dp_size - 1, 8, 128), jnp.float32),
        pltpu.VMEM((8, 128), jnp.float32),
        pltpu.SemaphoreType.DMA((count, dp_size)),
        pltpu.SemaphoreType.DMA((count, dp_size)),
        pltpu.SemaphoreType.DMA((count, dp_size)),
        pltpu.SemaphoreType.DMA((count, bits, dp_size // 2)),
        pltpu.SemaphoreType.DMA((count, bits, dp_size // 2)),
        pltpu.SemaphoreType.DMA((count, depth - 1)),
        pltpu.SemaphoreType.DMA((count, depth - 1)),
        pltpu.SemaphoreType.DMA((seq_size + dp_size - 2,)),
        pltpu.SemaphoreType.DMA((seq_size + dp_size - 2,)),
    ]
    shapes = [jax.ShapeDtypeStruct(tail, jnp.float32) for tail in tails]
    shapes.append(jax.ShapeDtypeStruct((8, 128), jnp.float32))
    return pl.pallas_call(
        functools.partial(scatter_kernel, dp_size, seq_size, count),
        out_shape=shapes,
        in_specs=[pl.BlockSpec(memory_space=pl.ANY)] * count,
        out_specs=[pl.BlockSpec(memory_space=pltpu.VMEM)] * (count + 1),
        scratch_shapes=scratch,
        compiler_params=pltpu.CompilerParams(
            collective_id=1, has_side_effects=True, vmem_limit_bytes=56 << 20
        ),
        name="scatter_all",
    )(*grads)


def layer_norm(values, gain_vec, shift_vec):
    centered = values - jnp.mean(values, axis=-1, keepdims=True)
    variance = jnp.mean(centered * centered, axis=-1, keepdims=True)
    return centered * lax.rsqrt(variance + norm_eps) * gain_vec + shift_vec


def slot_positions(slot_ids, order_table, block_len):
    block_ids = jnp.arange(order_table.shape[0], dtype=jnp.int32)
    one_hot = (slot_ids[:, None] // block_len == block_ids[None, :]).astype(jnp.int32)
    picked = jnp.sum(one_hot * order_table[None, :], axis=1)
    return picked * block_len + slot_ids % block_len


def contract_rows(left, right):
    return lax.dot_general(
        left, right, (((0,), (0,)), ((), ())), preferred_element_type=jnp.float32
    )


def contract_cols(left, right):
    return lax.dot_general(
        left, right, (((1,), (1,)), ((), ())), preferred_element_type=jnp.float32
    )


def masked_scores(queries, key_block, query_pos, key_pos, length, score_scale):
    scores = (
        jnp.einsum("qhd,khd->hqk", queries, key_block, preferred_element_type=jnp.float32)
        * score_scale
    )
    allowed = (key_pos[None, :] <= query_pos[:, None]) & (key_pos[None, :] < length)
    return jnp.where(allowed[None], scores, neg_fill)


def softmax_rows(queries, key_block, query_pos, key_pos, length, score_scale):
    scores = masked_scores(queries, key_block, query_pos, key_pos, length, score_scale)
    row_max = jnp.max(scores, axis=-1, keepdims=True)
    exp_scores = jnp.exp(scores - row_max)
    row_total = jnp.sum(exp_scores, axis=-1, keepdims=True)
    return (exp_scores / row_total, row_max + jnp.log(row_total))


def pack_small(vec_cols, bias, devices):
    wide = vec_cols.shape[1] // devices
    parts = vec_cols.reshape(8, devices, wide).transpose(1, 0, 2).reshape(devices, 8 * wide)
    flat = jnp.concatenate([parts, bias.reshape(devices, -1)], axis=1)
    length = flat.shape[1]
    padded = -(-length // 2048) * 2048
    flat = jnp.pad(flat, ((0, 0), (0, padded - length)))
    return flat.reshape(devices, padded // 128, 128)


def unpack_small(packed, devices, model_width, hidden):
    flat = packed.reshape(devices, -1)
    wide, high = model_width // devices, hidden // devices
    cols = flat[:, : 8 * wide].reshape(devices, 8, wide).transpose(1, 0, 2)
    return cols.reshape(8, model_width), flat[:, 8 * wide : 8 * wide + high].reshape(hidden)


def per_device(
    inputs,
    cotangent,
    lengths,
    block_order,
    step_count,
    learn_rates,
    w_qkv,
    w_proj,
    w_expand,
    w_shrink,
    vectors,
    bias_expand,
    first_qkv,
    first_proj,
    first_expand,
    first_shrink,
    first_vectors,
    first_bias,
    second_qkv,
    second_proj,
    second_expand,
    second_shrink,
    second_vectors,
    second_bias,
):
    low_type = jnp.bfloat16
    wide_type = jnp.float32
    dp_size, seq_size = lax.axis_size("dp"), lax.axis_size("seq")
    devices = dp_size * seq_size
    lead = (dp_size, seq_size // 2, 2)
    seqs_here, local_slots, model_width = inputs.shape
    hidden = w_expand.shape[1]
    total_slots = local_slots * seq_size
    block_len = total_slots // block_order.shape[0]
    score_scale = 1.0 / math.sqrt(HD)
    token_count = seqs_here * local_slots
    first_slot = lax.axis_index("seq") * local_slots
    local_pos = slot_positions(
        first_slot + jnp.arange(local_slots, dtype=jnp.int32), block_order, block_len
    )
    key_pos = slot_positions(jnp.arange(total_slots, dtype=jnp.int32), block_order, block_len)
    valid_rows = (local_pos[None, :] < lengths[:, None]).astype(wide_type)
    rows_in = inputs.reshape(token_count, model_width).astype(wide_type)

    small_block = pack_small(vectors.T, bias_expand, 1)[0].astype(low_type)
    gathered = gather_all(
        [
            small_block,
            w_qkv.astype(low_type),
            w_proj.astype(low_type),
            w_expand.astype(low_type),
            w_shrink.astype(low_type),
        ],
        dp_size,
        seq_size,
    )
    qkv_full = gathered[1].reshape(model_width, -1)
    proj_full = gathered[2].reshape(model_width, -1)
    expand_full = gathered[3].reshape(model_width, -1)
    shrink_full = gathered[4].reshape(hidden, -1)
    vec_cols, bias_full = unpack_small(
        gathered[0].astype(wide_type), devices, model_width, hidden
    )
    (
        gain_one,
        shift_one,
        bias_query,
        bias_value,
        bias_proj,
        gain_two,
        shift_two,
        bias_shrink,
    ) = [vec_cols[i] for i in range(8)]

    normed_one = layer_norm(rows_in, gain_one, shift_one).astype(low_type)
    bias_cat = jnp.concatenate([bias_query, jnp.zeros_like(bias_query), bias_value])
    qkv_rows = (jnp.dot(normed_one, qkv_full, preferred_element_type=wide_type) + bias_cat).astype(
        low_type
    )
    head_shape = (seqs_here, local_slots, HEADS, HD)
    query_all = qkv_rows[:, :model_width].reshape(head_shape)
    key_local = qkv_rows[:, model_width : 2 * model_width].reshape(head_shape)
    value_local = qkv_rows[:, 2 * model_width :].reshape(head_shape)
    keys_all, values_all = (
        lax.all_gather(key_local, "seq", axis=1, tiled=True),
        lax.all_gather(value_local, "seq", axis=1, tiled=True),
    )

    def forward_one(packed):
        queries, key_block, value_block, length = packed
        softmax_w, row_lse = softmax_rows(
            queries, key_block, local_pos, key_pos, length, score_scale
        )
        return jnp.einsum(
            "hqk,khd->qhd",
            softmax_w.astype(low_type),
            value_block,
            preferred_element_type=wide_type,
        )

    context = lax.map(forward_one, (query_all, keys_all, values_all, lengths))
    context_low = context.reshape(token_count, model_width).astype(low_type)
    attn_rows = jnp.dot(context_low, proj_full, preferred_element_type=wide_type) + bias_proj
    resid = rows_in + attn_rows
    normed_two = layer_norm(resid, gain_two, shift_two).astype(low_type)
    pre_act = jnp.dot(normed_two, expand_full, preferred_element_type=wide_type) + bias_full
    gelu_out, gelu_back = jax.vjp(lambda arg_in: jax.nn.gelu(arg_in, approximate=True), pre_act)
    act_low = gelu_out.astype(low_type)
    layer_rows = (
        resid + jnp.dot(act_low, shrink_full, preferred_element_type=wide_type) + bias_shrink
    )
    grad_rows = (cotangent.astype(wide_type) * valid_rows[:, :, None]).reshape(
        token_count, model_width
    )
    grad_low = grad_rows.astype(low_type)
    grad_shrink = contract_rows(act_low, grad_low)
    grad_bias_shrink = jnp.sum(grad_rows, axis=0)
    grad_act = contract_cols(grad_low, shrink_full)
    grad_pre = gelu_back(grad_act)[0].astype(low_type)
    grad_expand = contract_rows(normed_two, grad_pre)
    grad_bias_expand = jnp.sum(grad_pre, axis=0, dtype=wide_type)
    grad_normed_two = contract_cols(grad_pre, expand_full)
    norm_two_out, norm_back_two = jax.vjp(layer_norm, resid, gain_two, shift_two)
    grad_resid_part, grad_gain_two, grad_shift_two = norm_back_two(grad_normed_two)
    grad_resid = grad_rows + grad_resid_part
    grad_attn_low = grad_resid.astype(low_type)
    grad_proj = contract_rows(context_low, grad_attn_low)
    grad_bias_proj = jnp.sum(grad_attn_low, axis=0, dtype=wide_type)
    grad_context = contract_cols(grad_attn_low, proj_full).astype(low_type).reshape(head_shape)

    def backward_one(packed):
        queries, key_block, value_block, grad_ctx, length = packed
        softmax_w, row_lse = softmax_rows(
            queries, key_block, local_pos, key_pos, length, score_scale
        )
        grad_prob = jnp.einsum(
            "qhd,khd->hqk", grad_ctx, value_block, preferred_element_type=wide_type
        )
        delta = jnp.sum(softmax_w * grad_prob, axis=-1, keepdims=True)
        grad_score = (softmax_w * (grad_prob - delta)).astype(low_type)
        grad_query = (
            jnp.einsum("hqk,khd->qhd", grad_score, key_block, preferred_element_type=wide_type)
            * score_scale
        )
        key_terms = (
            jnp.einsum("hqk,qhd->khd", grad_score, queries, preferred_element_type=wide_type)
            * score_scale
        )
        value_terms = jnp.einsum(
            "hqk,qhd->khd", softmax_w.astype(low_type), grad_ctx, preferred_element_type=wide_type
        )
        return (grad_query, key_terms, value_terms)

    grad_query, key_terms, value_terms = lax.map(
        backward_one, (query_all, keys_all, values_all, grad_context, lengths)
    )
    key_sums, value_sums = (
        lax.psum_scatter(key_terms, "seq", scatter_dimension=1, tiled=True),
        lax.psum_scatter(value_terms, "seq", scatter_dimension=1, tiled=True),
    )
    grad_q_low = grad_query.reshape(token_count, model_width).astype(low_type)
    grad_v_low = value_sums.reshape(token_count, model_width).astype(low_type)
    grad_qkv_rows = jnp.concatenate(
        [grad_q_low, key_sums.reshape(token_count, model_width).astype(low_type), grad_v_low],
        axis=1,
    )
    grad_qkv_w = contract_rows(normed_one, grad_qkv_rows)
    grad_bias_query = jnp.sum(grad_q_low, axis=0, dtype=wide_type)
    grad_bias_value = jnp.sum(grad_v_low, axis=0, dtype=wide_type)
    grad_normed_one = contract_cols(grad_qkv_rows, qkv_full)
    norm_one_out, norm_back_one = jax.vjp(layer_norm, rows_in, gain_one, shift_one)
    grad_in_part, grad_gain_one, grad_shift_one = norm_back_one(grad_normed_one)
    grad_in_rows = grad_resid + grad_in_part
    grad_cols = jnp.stack(
        [
            grad_gain_one,
            grad_shift_one,
            grad_bias_query,
            grad_bias_value,
            grad_bias_proj,
            grad_gain_two,
            grad_shift_two,
            grad_bias_shrink,
        ],
        axis=0,
    )
    small_grad = pack_small(grad_cols, grad_bias_expand, devices)
    scattered = scatter_all(
        [
            grad_shrink.astype(low_type).reshape(lead + w_shrink.shape),
            grad_expand.astype(low_type).reshape(lead + w_expand.shape),
            grad_proj.astype(low_type).reshape(lead + w_proj.shape),
            grad_qkv_w.astype(low_type).reshape(lead + w_qkv.shape),
            small_grad.reshape(lead + small_grad.shape[1:]),
        ],
        dp_size,
        seq_size,
    )
    grad_shrink_mine, grad_expand_mine, grad_proj_mine, grad_qkv_mine, small_mine, squares = (
        scattered
    )
    vec_mine, grad_bias_mine = unpack_small(
        small_mine[None], 1, model_width // devices, hidden // devices
    )
    grad_vec_mine = vec_mine.T
    grads = (
        grad_qkv_mine,
        grad_proj_mine,
        grad_expand_mine,
        grad_shrink_mine,
        grad_vec_mine,
        grad_bias_mine,
    )
    masters = (w_qkv, w_proj, w_expand, w_shrink, vectors, bias_expand)
    firsts = (first_qkv, first_proj, first_expand, first_shrink, first_vectors, first_bias)
    seconds = (second_qkv, second_proj, second_expand, second_shrink, second_vectors, second_bias)
    grad_norm = jnp.sqrt(jnp.sum(squares))
    clip_factor = clip_bound / jnp.maximum(grad_norm, clip_bound)
    step_float = step_count.astype(wide_type)
    correct_first = 1.0 - beta_first**step_float
    correct_second = 1.0 - beta_second**step_float
    renewed = []
    first_new = []
    second_new = []
    for group_id in range(6):
        clipped = grads[group_id] * clip_factor
        moment_one = beta_first * firsts[group_id] + (1.0 - beta_first) * clipped
        moment_two = beta_second * seconds[group_id] + (1.0 - beta_second) * clipped * clipped
        update = moment_one / correct_first / (jnp.sqrt(moment_two / correct_second) + adam_eps)
        if group_id < 4:
            update = update + decay_rate * masters[group_id]
        renewed.append(masters[group_id] - learn_rates[group_id] * update)
        first_new.append(moment_one)
        second_new.append(moment_two)
    layer_out = layer_rows.reshape(seqs_here, local_slots, model_width)
    grad_inputs = grad_in_rows.reshape(seqs_here, local_slots, model_width)
    return (
        (layer_out, grad_inputs, grad_norm) + tuple(renewed) + tuple(first_new) + tuple(second_new)
    )


def solution(mesh):
    token_spec = P("dp", "seq", None)
    matrix_spec = P(("dp", "seq"), None)
    row_spec = P(("dp", "seq"))
    group = (matrix_spec,) * 5 + (row_spec,)
    return jax.shard_map(
        per_device,
        mesh=mesh,
        in_specs=(token_spec, token_spec, P("dp"), P(), P(), P()) + group * 3,
        out_specs=(token_spec, token_spec, P()) + group * 3,
        check_vma=False,
    )
```

```python
import functools

import jax
import jax.numpy as jnp
from jax import lax
from jax.experimental import pallas as pl
from jax.experimental.pallas import tpu as pltpu
from jax.sharding import PartitionSpec as P

HEADS = 16
HD = 64
MESH = pl.DeviceIdType.MESH


norm_eps = 1e-05
neg_fill = -1e30
beta_first = 0.9
beta_second = 0.95
adam_eps = 1e-08
decay_rate = 0.1
clip_bound = 1.0


def flip(index, mask):
    return index + mask * (1 - 2 * ((index // mask) % 2))


class Place:
    def __init__(self, dp_size, seq_size):
        self.dp_size = dp_size
        self.depth = seq_size // 2
        self.bits = dp_size.bit_length() - 1
        self.dp = lax.axis_index("dp")
        seq = lax.axis_index("seq")
        self.z = seq // 2
        self.core = seq % 2
        self.masks = self.masks_of(self.core)

    def masks_of(self, core):
        return [
            (1 - core) * 2 ** (k % self.bits) + core * 2 ** ((k + 1) % self.bits)
            for k in range(self.bits)
        ]

    def leaving(self, core_masks=None):
        masks = self.masks if core_masks is None else core_masks
        order = []
        for k in range(self.bits - 1, -1, -1):
            order = order + self.span(flip(self.dp, masks[k]), k, masks)
        return order + [self.dp]

    def cube(self, k):
        return (flip(self.dp, self.masks[k]), self.z * 2 + self.core)

    def span(self, start, k, masks=None):
        found = [start]
        for mask in (self.masks if masks is None else masks)[:k]:
            found = found + [flip(one, mask) for one in found]
        return found

    def sibling(self):
        return (self.dp, self.z * 2 + 1 - self.core)

    def line(self, j):
        return (self.dp, ((self.z + j) % self.depth) * 2 + self.core)


def greet(peers):
    barrier = pltpu.get_barrier_semaphore()
    for peer in peers:
        pl.semaphore_signal(barrier, inc=1, device_id=peer, device_id_type=MESH)
    pl.semaphore_wait(barrier, len(peers))


def gather_kernel(dp_size, seq_size, count, *refs):
    sources, fulls = refs[:count], refs[count : 2 * count]
    local_sem, line_send, cube_send, pair_send, arrive = refs[2 * count :]
    at = Place(dp_size, seq_size)
    depth, bits, dp, z, core = at.depth, at.bits, at.dp, at.z, at.core
    greet(
        [at.line(j) for j in range(1, depth)] + [at.cube(k) for k in range(bits)] + [at.sibling()]
    )
    pending = []

    def send(a, source, row, level, peer, sem):
        copy = pltpu.make_async_remote_copy(
            src_ref=source,
            dst_ref=fulls[a].at[row, level, core],
            send_sem=sem,
            recv_sem=arrive.at[a, row, level, core],
            device_id=peer,
            device_id_type=MESH,
        )
        copy.start()
        pending.append(copy)

    def received(a, row, level, side):
        block = fulls[a].at[row, level, side]
        pltpu.make_async_copy(block, block, arrive.at[a, row, level, side]).wait()

    def pass_on(a, source, row, slot, level, first):
        for k in range(first, bits):
            send(a, source, row, level, at.cube(k), cube_send.at[a, k, slot, level])
        send(a, source, row, level, at.sibling(), pair_send.at[a, slot, level])

    for a in range(count):
        for j in range(1, depth):
            send(a, sources[a], dp, z, at.line(j), line_send.at[a, j - 1])
        pass_on(a, sources[a], dp, 0, z, 0)
    locals_ = []
    for a in range(count):
        copy = pltpu.make_async_copy(sources[a], fulls[a].at[dp, z, core], local_sem.at[a])
        copy.start()
        locals_.append(copy)

    def line_stage(a):
        for j in range(depth - 1, 0, -1):
            level = (z + j) % depth
            received(a, dp, level, core)
            pass_on(a, fulls[a].at[dp, level, core], dp, 0, level, 0)

    def cube_stage(a, k):
        for slot, row in enumerate(at.span(flip(dp, at.masks[k]), k)):
            for j in range(depth):
                level = (z + j) % depth
                received(a, row, level, core)
                pass_on(a, fulls[a].at[row, level, core], row, 2**k + slot, level, k + 1)

    stages = bits + 1
    for step in range(count + stages - 1):
        for stage in range(stages):
            a = step - stage
            if 0 <= a < count:
                if stage == 0:
                    line_stage(a)
                else:
                    cube_stage(a, stage - 1)
    for a in range(count):
        for row in range(dp_size):
            for level in range(depth):
                received(a, row, level, 1 - core)
    for copy in locals_:
        copy.wait()
    for copy in pending:
        copy.wait_send()


def gather_all(blocks, dp_size, seq_size):
    count = len(blocks)
    depth, bits = seq_size // 2, dp_size.bit_length() - 1
    shapes = [
        jax.ShapeDtypeStruct((dp_size, depth, 2) + block.shape, block.dtype) for block in blocks
    ]
    return pl.pallas_call(
        functools.partial(gather_kernel, dp_size, seq_size, count),
        out_shape=shapes,
        in_specs=[pl.BlockSpec(memory_space=pl.ANY)] * count,
        out_specs=[pl.BlockSpec(memory_space=pl.ANY)] * count,
        scratch_shapes=[
            pltpu.SemaphoreType.DMA((count,)),
            pltpu.SemaphoreType.DMA((count, depth - 1)),
            pltpu.SemaphoreType.DMA((count, bits, dp_size, depth)),
            pltpu.SemaphoreType.DMA((count, dp_size, depth)),
            pltpu.SemaphoreType.DMA((count, dp_size, depth, 2)),
        ],
        compiler_params=pltpu.CompilerParams(collective_id=0, has_side_effects=True),
        name="gather_all",
    )(*blocks)


def scatter_kernel(dp_size, seq_size, count, *refs):
    at = Place(dp_size, seq_size)
    depth, bits, dp, z, core = at.depth, at.bits, at.dp, at.z, at.core
    grads, outs, norm_out = refs[:count], refs[count : 2 * count], refs[2 * count]
    scratch = refs[2 * count + 1 :]
    own, pair = scratch[:count], scratch[count : 2 * count]
    cube = [scratch[(2 + k) * count : (3 + k) * count] for k in range(bits)]
    line = scratch[(2 + bits) * count : (3 + bits) * count]
    seq_part, dp_part, mine = scratch[(3 + bits) * count : (3 + bits) * count + 3]
    (own_sem, pair_send, pair_recv, cube_send, cube_recv, line_send, line_recv) = scratch[
        (3 + bits) * count + 3 : (3 + bits) * count + 10
    ]
    norm_send, norm_recv = scratch[(3 + bits) * count + 10 :]
    seq = z * 2 + core
    seq_peers = [(dp, (seq + j) % seq_size) for j in range(1, seq_size)]
    dp_peers = [((dp + j) % dp_size, seq) for j in range(1, dp_size)]
    greet(seq_peers + dp_peers)
    pending = []

    order = at.leaving()
    theirs = at.leaving(at.masks_of(1 - core))
    for a in range(count):
        for spot, row in enumerate(order):
            copy = pltpu.make_async_remote_copy(
                src_ref=grads[a].at[theirs[spot], :, 1 - core],
                dst_ref=pair[a].at[theirs[spot]],
                send_sem=pair_send.at[a, spot],
                recv_sem=pair_recv.at[a, theirs[spot]],
                device_id=at.sibling(),
                device_id_type=MESH,
            )
            copy.start()
            pending.append(copy)
            pltpu.make_async_copy(
                grads[a].at[row, :, core], own[a].at[row], own_sem.at[a, spot]
            ).start()

    def ready(a, spot):
        row = order[spot]
        pltpu.make_async_copy(grads[a].at[row, :, core], own[a].at[row], own_sem.at[a, spot]).wait()
        pltpu.make_async_copy(pair[a].at[row], pair[a].at[row], pair_recv.at[a, row]).wait()

    def total(a, row, level, rows, hops):
        value = own[a][row, level, rows].astype(jnp.float32)
        value = value + pair[a][row, level, rows].astype(jnp.float32)
        for k, slot in hops:
            value = value + cube[k][a][slot, level, rows].astype(jnp.float32)
        return value

    def each_chunk(a, body):
        height = own[a].shape[2]
        step = min(16, height)
        if step == height:
            body(pl.ds(0, step))
        else:

            def one(i, carry):
                body(pl.ds(pl.multiple_of(i * step, step), step))
                return carry

            lax.fori_loop(0, height // step, one, 0)

    def fold(a, row, hops):
        for level in range(depth):

            def body(rows, level=level):
                own[a][row, level, rows] = total(a, row, level, rows, hops).astype(own[a].dtype)

            each_chunk(a, body)

    def cube_stage(a, k):
        leave = at.span(flip(dp, at.masks[k]), k)
        for slot, row in enumerate(leave):
            spot = spot_of(bits, k, slot)
            ready(a, spot)
            landed = [(q, landing_slot(bits, k, slot, q)) for q in range(k + 1, bits)]
            for q, hop_slot in landed:
                block = cube[q][a].at[hop_slot]
                pltpu.make_async_copy(block, block, cube_recv.at[a, q, hop_slot]).wait()
            fold(a, row, landed)
            copy = pltpu.make_async_remote_copy(
                src_ref=own[a].at[row],
                dst_ref=cube[k][a].at[slot],
                send_sem=cube_send.at[a, k, slot],
                recv_sem=cube_recv.at[a, k, slot],
                device_id=at.cube(k),
                device_id_type=MESH,
            )
            copy.start()
            pending.append(copy)

    all_hops = [(q, 0) for q in range(bits)]

    def line_stage(a):
        ready(a, len(order) - 1)
        for q, hop_slot in all_hops:
            block = cube[q][a].at[hop_slot]
            pltpu.make_async_copy(block, block, cube_recv.at[a, q, hop_slot]).wait()
        for j in range(1, depth):
            level = (z + j) % depth

            def body(rows, level=level):
                own[a][dp, level, rows] = total(a, dp, level, rows, all_hops).astype(own[a].dtype)

            each_chunk(a, body)
            copy = pltpu.make_async_remote_copy(
                src_ref=own[a].at[dp, level],
                dst_ref=line[a].at[j - 1],
                send_sem=line_send.at[a, j - 1],
                recv_sem=line_recv.at[a, j - 1],
                device_id=at.line(j),
                device_id_type=MESH,
            )
            copy.start()
            pending.append(copy)

    mine[...] = jnp.zeros_like(mine)

    def final_stage(a):
        for j in range(1, depth):
            block = line[a].at[j - 1]
            pltpu.make_async_copy(block, block, line_recv.at[a, j - 1]).wait()

        def body(rows):
            value = total(a, dp, z, rows, all_hops)
            for j in range(1, depth):
                value = value + line[a][j - 1, rows].astype(jnp.float32)
            outs[a][rows] = value
            squares = value * value
            height, width = squares.shape
            folded = squares.reshape(height // 8, 8, width).sum(0)
            part = folded[:, :128]
            for lane in range(1, width // 128):
                part = part + folded[:, lane * 128 : (lane + 1) * 128]
            mine[...] += part

        each_chunk(a, body)

    stages = bits + 2
    for step in range(count + stages - 1):
        for stage in range(stages):
            a = step - stage
            if 0 <= a < count:
                if stage < bits:
                    cube_stage(a, bits - 1 - stage)
                elif stage == bits:
                    line_stage(a)
                else:
                    final_stage(a)

    def exchange(peers, parts, base):
        copies = []
        for i, peer in enumerate(peers):
            copy = pltpu.make_async_remote_copy(
                src_ref=mine,
                dst_ref=parts.at[i],
                send_sem=norm_send.at[base + i],
                recv_sem=norm_recv.at[base + i],
                device_id=peer,
                device_id_type=MESH,
            )
            copy.start()
            copies.append(copy)
        for copy in copies:
            copy.wait()

    exchange(seq_peers, seq_part, 0)
    value = mine[...]
    for i in range(seq_size - 1):
        value = value + seq_part[i]
    mine[...] = value
    exchange(dp_peers, dp_part, seq_size - 1)
    value = mine[...]
    for i in range(dp_size - 1):
        value = value + dp_part[i]
    norm_out[...] = value
    for copy in pending:
        copy.wait_send()


def spot_of(bits, k, slot):
    return sum(2**q for q in range(k + 1, bits)) + slot


def landing_slot(bits, k, slot, q):
    return 2**k + slot


def scatter_all(grads, dp_size, seq_size):
    count = len(grads)
    depth, bits = seq_size // 2, dp_size.bit_length() - 1
    tails = [grad.shape[3:] for grad in grads]
    kinds = [grad.dtype for grad in grads]
    scratch = []
    for lead in [(dp_size, depth)] * 2 + [(2**k, depth) for k in range(bits)] + [(depth - 1,)]:
        scratch += [pltpu.VMEM(lead + tail, kind) for tail, kind in zip(tails, kinds)]
    scratch += [
        pltpu.VMEM((seq_size - 1, 8, 128), jnp.float32),
        pltpu.VMEM((dp_size - 1, 8, 128), jnp.float32),
        pltpu.VMEM((8, 128), jnp.float32),
        pltpu.SemaphoreType.DMA((count, dp_size)),
        pltpu.SemaphoreType.DMA((count, dp_size)),
        pltpu.SemaphoreType.DMA((count, dp_size)),
        pltpu.SemaphoreType.DMA((count, bits, dp_size // 2)),
        pltpu.SemaphoreType.DMA((count, bits, dp_size // 2)),
        pltpu.SemaphoreType.DMA((count, depth - 1)),
        pltpu.SemaphoreType.DMA((count, depth - 1)),
        pltpu.SemaphoreType.DMA((seq_size + dp_size - 2,)),
        pltpu.SemaphoreType.DMA((seq_size + dp_size - 2,)),
    ]
    shapes = [jax.ShapeDtypeStruct(tail, jnp.float32) for tail in tails]
    shapes.append(jax.ShapeDtypeStruct((8, 128), jnp.float32))
    return pl.pallas_call(
        functools.partial(scatter_kernel, dp_size, seq_size, count),
        out_shape=shapes,
        in_specs=[pl.BlockSpec(memory_space=pl.ANY)] * count,
        out_specs=[pl.BlockSpec(memory_space=pltpu.VMEM)] * (count + 1),
        scratch_shapes=scratch,
        compiler_params=pltpu.CompilerParams(
            collective_id=1, has_side_effects=True, vmem_limit_bytes=56 << 20
        ),
        name="scatter_all",
    )(*grads)


class Heads:
    def __init__(self, seq_size, pairs, seqs):
        self.seq_size, self.pairs = seq_size, pairs
        self.units = seqs * pairs // seq_size
        self.dp = lax.axis_index("dp")
        self.seq = lax.axis_index("seq")
        self.peers = [(self.seq + j) % seq_size for j in range(1, seq_size)]

    def share(self, seq):
        return seq % self.pairs, pl.ds((seq // self.pairs) * self.units, self.units)

    def to_heads(self, rows, units, local_sem, send_sem, recv_sem):
        copies = []
        for j, peer in enumerate(self.peers):
            pair, which = self.share(peer)
            copies.append(
                pltpu.make_async_remote_copy(
                    src_ref=rows.at[:, pair, which],
                    dst_ref=units.at[:, :, self.seq],
                    send_sem=send_sem.at[j],
                    recv_sem=recv_sem.at[j],
                    device_id=(self.dp, peer),
                    device_id_type=MESH,
                )
            )
        pair, which = self.share(self.seq)
        copies.append(
            pltpu.make_async_copy(rows.at[:, pair, which], units.at[:, :, self.seq], local_sem)
        )
        for copy in copies:
            copy.start()
        return copies

    def to_rows(self, units, rows, local_sem, send_sem, recv_sem):
        copies = []
        pair, which = self.share(self.seq)
        for j, peer in enumerate(self.peers):
            copies.append(
                pltpu.make_async_remote_copy(
                    src_ref=units.at[:, :, peer],
                    dst_ref=rows.at[:, pair, which],
                    send_sem=send_sem.at[j],
                    recv_sem=recv_sem.at[j],
                    device_id=(self.dp, peer),
                    device_id_type=MESH,
                )
            )
        copies.append(
            pltpu.make_async_copy(units.at[:, :, self.seq], rows.at[:, pair, which], local_sem)
        )
        for copy in copies:
            copy.start()
        return copies

    def unit_sequence(self, unit):
        return (self.seq // self.pairs) * self.units + unit


def head_lanes(rows, head):
    lane = lax.broadcasted_iota(jnp.int32, rows.shape, 1)
    return jnp.where(lane // HD == head, rows, jnp.zeros_like(rows))


CHUNK = 256


def attend(heads, qkv, key_pos, query_pos, context, stats):
    units, length = context.shape[0], query_pos.shape[1]
    tall = qkv.shape[2] * qkv.shape[3]
    for unit in range(units):
        keys = qkv[1, unit].reshape(tall, 128)
        values_t = qkv[2, unit].reshape(tall, 128).T
        pos = key_pos[heads.unit_sequence(unit)][:, :1]

        def chunk(i, carry, unit=unit, keys=keys, values_t=values_t, pos=pos):
            where = pl.ds(pl.multiple_of(i * CHUNK, CHUNK), CHUNK)
            queries = context_rows(qkv.at[0, unit], where) * 0.125
            allowed = pos <= query_pos[:, where]
            halves = []
            for head in range(2):
                scores = contract_cols(keys, head_lanes(queries, head))
                scores = jnp.where(allowed, scores, neg_fill)
                top = jnp.max(scores, axis=0, keepdims=True)
                exp_scores = jnp.exp(scores - top)
                total = jnp.sum(exp_scores, axis=0, keepdims=True)
                weights = (exp_scores * (1.0 / total)).astype(jnp.bfloat16)
                stats[unit, head, :, where] = top + jnp.log(total)
                halves.append(
                    jnp.dot(
                        values_t[head * HD : (head + 1) * HD],
                        weights,
                        preferred_element_type=jnp.float32,
                    )
                )
            rows = jnp.concatenate(halves, axis=0).T.astype(jnp.bfloat16)
            store_rows(context.at[unit], where, rows)
            return carry

        lax.fori_loop(0, length // CHUNK, chunk, 0)


def context_rows(ref, where):
    slots = ref.shape[1]
    some = ref[pl.ds(where.start // slots, CHUNK // slots)]
    return some.reshape(CHUNK, 128)


def store_rows(ref, where, rows):
    slots = ref.shape[1]
    ref[pl.ds(where.start // slots, CHUNK // slots)] = rows.reshape(CHUNK // slots, slots, 128)


def attend_back(heads, qkv, grad_ctx, key_pos, query_pos, stats, grads, key_sum, value_sum):
    units, length = grad_ctx.shape[0], query_pos.shape[1]
    tall = qkv.shape[2] * qkv.shape[3]
    for unit in range(units):
        keys = qkv[1, unit].reshape(tall, 128)
        keys_t = keys.T
        values = qkv[2, unit].reshape(tall, 128)
        pos = key_pos[heads.unit_sequence(unit)][:, :1]
        key_sum[...] = jnp.zeros_like(key_sum)
        value_sum[...] = jnp.zeros_like(value_sum)

        def chunk(i, carry, unit=unit, keys=keys, keys_t=keys_t, values=values, pos=pos):
            where = pl.ds(pl.multiple_of(i * CHUNK, CHUNK), CHUNK)
            queries = context_rows(qkv.at[0, unit], where) * 0.125
            grad_rows = context_rows(grad_ctx.at[unit], where)
            allowed = pos <= query_pos[:, where]
            halves = []
            for head in range(2):
                queries_h = head_lanes(queries, head)
                grad_h = head_lanes(grad_rows, head)
                scores = jnp.where(allowed, contract_cols(keys, queries_h), neg_fill)
                weights = jnp.exp(scores - stats[unit, head, :, where])
                grad_prob = contract_cols(values, grad_h)
                delta = jnp.sum(weights * grad_prob, axis=0, keepdims=True)
                grad_score = (weights * (grad_prob - delta)).astype(jnp.bfloat16)
                value_sum[...] += jnp.dot(
                    weights.astype(jnp.bfloat16), grad_h, preferred_element_type=jnp.float32
                )
                key_sum[...] += jnp.dot(
                    grad_score, queries_h, preferred_element_type=jnp.float32
                )
                halves.append(
                    jnp.dot(
                        keys_t[head * HD : (head + 1) * HD],
                        grad_score,
                        preferred_element_type=jnp.float32,
                    )
                )
            rows = (jnp.concatenate(halves, axis=0).T * 0.125).astype(jnp.bfloat16)
            store_rows(grads.at[0, unit], where, rows)
            return carry

        lax.fori_loop(0, length // CHUNK, chunk, 0)
        shape = grads.shape[2:]
        grads[1, unit] = key_sum[...].astype(jnp.bfloat16).reshape(shape)
        grads[2, unit] = value_sum[...].astype(jnp.bfloat16).reshape(shape)


def forward_kernel(
    seq_size,
    seqs,
    rows,
    key_pos,
    query_pos,
    context_rows_out,
    qkv,
    stats,
    context,
    local_sem,
    send_sem,
    recv_sem,
):
    heads = Heads(seq_size, rows.shape[1], seqs)
    greet([(heads.dp, peer) for peer in heads.peers])
    for copy in heads.to_heads(rows, qkv, local_sem.at[0], send_sem.at[0], recv_sem.at[0]):
        copy.wait()
    attend(heads, qkv, key_pos, query_pos, context.at[0], stats)
    for copy in heads.to_rows(
        context, context_rows_out, local_sem.at[1], send_sem.at[1], recv_sem.at[1]
    ):
        copy.wait()


def backward_kernel(
    seq_size,
    seqs,
    rows,
    qkv,
    stats,
    key_pos,
    query_pos,
    grad_rows_out,
    grad_ctx,
    grads,
    key_sum,
    value_sum,
    local_sem,
    send_sem,
    recv_sem,
):
    heads = Heads(seq_size, rows.shape[1], seqs)
    greet([(heads.dp, peer) for peer in heads.peers])
    for copy in heads.to_heads(rows, grad_ctx, local_sem.at[0], send_sem.at[0], recv_sem.at[0]):
        copy.wait()
    attend_back(
        heads, qkv, grad_ctx.at[0], key_pos, query_pos, stats, grads, key_sum, value_sum
    )
    for copy in heads.to_rows(
        grads, grad_rows_out, local_sem.at[1], send_sem.at[1], recv_sem.at[1]
    ):
        copy.wait()


def exchange_sems(seq_size):
    return [
        pltpu.SemaphoreType.DMA((2,)),
        pltpu.SemaphoreType.DMA((2, seq_size - 1)),
        pltpu.SemaphoreType.DMA((2, seq_size - 1)),
    ]


VMEM_SPEC = pl.BlockSpec(memory_space=pltpu.VMEM)


def attention_forward(rows, key_pos, query_pos, seq_size):
    pairs, seqs, slots = rows.shape[1:4]
    units = seqs * pairs // seq_size
    shapes = [
        jax.ShapeDtypeStruct((1,) + rows.shape[1:], rows.dtype),
        jax.ShapeDtypeStruct((3, units, seq_size, slots, 128), rows.dtype),
        jax.ShapeDtypeStruct((units, 2, 1, seq_size * slots), jnp.float32),
    ]
    return pl.pallas_call(
        functools.partial(forward_kernel, seq_size, seqs),
        out_shape=shapes,
        in_specs=[VMEM_SPEC] * 3,
        out_specs=[VMEM_SPEC] * 3,
        scratch_shapes=[pltpu.VMEM((1, units, seq_size, slots, 128), rows.dtype)]
        + exchange_sems(seq_size),
        compiler_params=pltpu.CompilerParams(
            collective_id=2, has_side_effects=True, vmem_limit_bytes=40 << 20
        ),
        name="attention_forward",
    )(rows, key_pos, query_pos)


def attention_backward(rows, qkv, stats, key_pos, query_pos, seq_size):
    pairs, seqs, slots = rows.shape[1:4]
    units = seqs * pairs // seq_size
    length = seq_size * slots
    return pl.pallas_call(
        functools.partial(backward_kernel, seq_size, seqs),
        out_shape=jax.ShapeDtypeStruct((3,) + rows.shape[1:], rows.dtype),
        in_specs=[VMEM_SPEC] * 5,
        out_specs=VMEM_SPEC,
        scratch_shapes=[
            pltpu.VMEM((1, units, seq_size, slots, 128), rows.dtype),
            pltpu.VMEM((3, units, seq_size, slots, 128), rows.dtype),
            pltpu.VMEM((length, 128), jnp.float32),
            pltpu.VMEM((length, 128), jnp.float32),
        ]
        + exchange_sems(seq_size),
        compiler_params=pltpu.CompilerParams(
            collective_id=3, has_side_effects=True, vmem_limit_bytes=40 << 20
        ),
        name="attention_backward",
    )(rows, qkv, stats, key_pos, query_pos)


def contract_rows(left, right):
    return lax.dot_general(
        left, right, (((0,), (0,)), ((), ())), preferred_element_type=jnp.float32
    )


def contract_cols(left, right):
    return lax.dot_general(
        left, right, (((1,), (1,)), ((), ())), preferred_element_type=jnp.float32
    )


def layer_norm(values, gain_vec, shift_vec):
    centered = values - jnp.mean(values, axis=-1, keepdims=True)
    variance = jnp.mean(centered * centered, axis=-1, keepdims=True)
    return centered * lax.rsqrt(variance + norm_eps) * gain_vec + shift_vec


def slot_positions(slot_ids, order_table, block_len):
    block_ids = jnp.arange(order_table.shape[0], dtype=jnp.int32)
    one_hot = (slot_ids[:, None] // block_len == block_ids[None, :]).astype(jnp.int32)
    picked = jnp.sum(one_hot * order_table[None, :], axis=1)
    return picked * block_len + slot_ids % block_len


def pack_small(vec_cols, bias, devices):
    wide = vec_cols.shape[1] // devices
    parts = vec_cols.reshape(8, devices, wide).transpose(1, 0, 2).reshape(devices, 8 * wide)
    flat = jnp.concatenate([parts, bias.reshape(devices, -1)], axis=1)
    length = flat.shape[1]
    padded = -(-length // 2048) * 2048
    flat = jnp.pad(flat, ((0, 0), (0, padded - length)))
    return flat.reshape(devices, padded // 128, 128)


def unpack_small(packed, devices, model_width, hidden):
    flat = packed.reshape(devices, -1)
    wide, high = model_width // devices, hidden // devices
    cols = flat[:, : 8 * wide].reshape(devices, 8, wide).transpose(1, 0, 2)
    return cols.reshape(8, model_width), flat[:, 8 * wide : 8 * wide + high].reshape(hidden)


def per_device(
    inputs,
    cotangent,
    lengths,
    block_order,
    step_count,
    learn_rates,
    w_qkv,
    w_proj,
    w_expand,
    w_shrink,
    vectors,
    bias_expand,
    first_qkv,
    first_proj,
    first_expand,
    first_shrink,
    first_vectors,
    first_bias,
    second_qkv,
    second_proj,
    second_expand,
    second_shrink,
    second_vectors,
    second_bias,
):
    low_type = jnp.bfloat16
    wide_type = jnp.float32
    dp_size, seq_size = lax.axis_size("dp"), lax.axis_size("seq")
    devices = dp_size * seq_size
    lead = (dp_size, seq_size // 2, 2)
    seqs_here, local_slots, model_width = inputs.shape
    hidden = w_expand.shape[1]
    total_slots = local_slots * seq_size
    block_len = total_slots // block_order.shape[0]
    token_count = seqs_here * local_slots
    first_slot = lax.axis_index("seq") * local_slots
    local_pos = slot_positions(
        first_slot + jnp.arange(local_slots, dtype=jnp.int32), block_order, block_len
    )
    key_pos = slot_positions(jnp.arange(total_slots, dtype=jnp.int32), block_order, block_len)
    valid_rows = (local_pos[None, :] < lengths[:, None]).astype(wide_type)
    rows_in = inputs.reshape(token_count, model_width).astype(wide_type)

    small_block = pack_small(vectors.T, bias_expand, 1)[0].astype(low_type)
    gathered = gather_all(
        [
            small_block,
            w_qkv.astype(low_type),
            w_proj.astype(low_type),
            w_expand.astype(low_type),
            w_shrink.astype(low_type),
        ],
        dp_size,
        seq_size,
    )
    qkv_full = gathered[1].reshape(model_width, -1)
    proj_full = gathered[2].reshape(model_width, -1)
    expand_full = gathered[3].reshape(model_width, -1)
    shrink_full = gathered[4].reshape(hidden, -1)
    vec_cols, bias_full = unpack_small(
        gathered[0].astype(wide_type), devices, model_width, hidden
    )
    (
        gain_one,
        shift_one,
        bias_query,
        bias_value,
        bias_proj,
        gain_two,
        shift_two,
        bias_shrink,
    ) = [vec_cols[i] for i in range(8)]

    normed_one = layer_norm(rows_in, gain_one, shift_one).astype(low_type)
    bias_cat = jnp.concatenate([bias_query, jnp.zeros_like(bias_query), bias_value])
    qkv_rows = (jnp.dot(normed_one, qkv_full, preferred_element_type=wide_type) + bias_cat).astype(
        low_type
    )
    pairs = HEADS // 2
    row_shape = (seqs_here, local_slots, -1, pairs, 128)
    qkv_heads = qkv_rows.reshape(row_shape).transpose(2, 3, 0, 1, 4)
    far = jnp.where(key_pos[None, :] < lengths[:, None], key_pos[None, :], 2**30)
    key_limits = jnp.broadcast_to(far[:, :, None], (seqs_here, total_slots, 128))
    query_row = key_pos[None, :]
    context, qkv_units, row_stats = attention_forward(
        qkv_heads, key_limits, query_row, seq_size
    )
    context_low = context[0].transpose(1, 2, 0, 3).reshape(token_count, model_width)
    attn_rows = jnp.dot(context_low, proj_full, preferred_element_type=wide_type) + bias_proj
    resid = rows_in + attn_rows
    normed_two = layer_norm(resid, gain_two, shift_two).astype(low_type)
    pre_act = jnp.dot(normed_two, expand_full, preferred_element_type=wide_type) + bias_full
    gelu_out, gelu_back = jax.vjp(lambda arg_in: jax.nn.gelu(arg_in, approximate=True), pre_act)
    act_low = gelu_out.astype(low_type)
    layer_rows = (
        resid + jnp.dot(act_low, shrink_full, preferred_element_type=wide_type) + bias_shrink
    )
    grad_rows = (cotangent.astype(wide_type) * valid_rows[:, :, None]).reshape(
        token_count, model_width
    )
    grad_low = grad_rows.astype(low_type)
    grad_shrink = contract_rows(act_low, grad_low)
    grad_bias_shrink = jnp.sum(grad_rows, axis=0)
    grad_act = contract_cols(grad_low, shrink_full)
    grad_pre = gelu_back(grad_act)[0].astype(low_type)
    grad_expand = contract_rows(normed_two, grad_pre)
    grad_bias_expand = jnp.sum(grad_pre, axis=0, dtype=wide_type)
    grad_normed_two = contract_cols(grad_pre, expand_full)
    norm_two_out, norm_back_two = jax.vjp(layer_norm, resid, gain_two, shift_two)
    grad_resid_part, grad_gain_two, grad_shift_two = norm_back_two(grad_normed_two)
    grad_resid = grad_rows + grad_resid_part
    grad_attn_low = grad_resid.astype(low_type)
    grad_proj = contract_rows(context_low, grad_attn_low)
    grad_bias_proj = jnp.sum(grad_attn_low, axis=0, dtype=wide_type)
    grad_context = contract_cols(grad_attn_low, proj_full).astype(low_type)
    grad_context = grad_context.reshape(row_shape).transpose(2, 3, 0, 1, 4)
    grad_heads = attention_backward(
        grad_context, qkv_units, row_stats, key_limits, query_row, seq_size
    )
    grad_qkv_rows = grad_heads.transpose(2, 3, 0, 1, 4).reshape(token_count, 3 * model_width)
    grad_q_low = grad_qkv_rows[:, :model_width]
    grad_v_low = grad_qkv_rows[:, 2 * model_width :]
    grad_qkv_w = contract_rows(normed_one, grad_qkv_rows)
    grad_bias_query = jnp.sum(grad_q_low, axis=0, dtype=wide_type)
    grad_bias_value = jnp.sum(grad_v_low, axis=0, dtype=wide_type)
    grad_normed_one = contract_cols(grad_qkv_rows, qkv_full)
    norm_one_out, norm_back_one = jax.vjp(layer_norm, rows_in, gain_one, shift_one)
    grad_in_part, grad_gain_one, grad_shift_one = norm_back_one(grad_normed_one)
    grad_in_rows = grad_resid + grad_in_part
    grad_cols = jnp.stack(
        [
            grad_gain_one,
            grad_shift_one,
            grad_bias_query,
            grad_bias_value,
            grad_bias_proj,
            grad_gain_two,
            grad_shift_two,
            grad_bias_shrink,
        ],
        axis=0,
    )
    small_grad = pack_small(grad_cols, grad_bias_expand, devices)
    scattered = scatter_all(
        [
            grad_shrink.astype(low_type).reshape(lead + w_shrink.shape),
            grad_expand.astype(low_type).reshape(lead + w_expand.shape),
            grad_proj.astype(low_type).reshape(lead + w_proj.shape),
            grad_qkv_w.astype(low_type).reshape(lead + w_qkv.shape),
            small_grad.reshape(lead + small_grad.shape[1:]),
        ],
        dp_size,
        seq_size,
    )
    grad_shrink_mine, grad_expand_mine, grad_proj_mine, grad_qkv_mine, small_mine, squares = (
        scattered
    )
    vec_mine, grad_bias_mine = unpack_small(
        small_mine[None], 1, model_width // devices, hidden // devices
    )
    grad_vec_mine = vec_mine.T
    grads = (
        grad_qkv_mine,
        grad_proj_mine,
        grad_expand_mine,
        grad_shrink_mine,
        grad_vec_mine,
        grad_bias_mine,
    )
    masters = (w_qkv, w_proj, w_expand, w_shrink, vectors, bias_expand)
    firsts = (first_qkv, first_proj, first_expand, first_shrink, first_vectors, first_bias)
    seconds = (second_qkv, second_proj, second_expand, second_shrink, second_vectors, second_bias)
    grad_norm = jnp.sqrt(jnp.sum(squares))
    clip_factor = clip_bound / jnp.maximum(grad_norm, clip_bound)
    step_float = step_count.astype(wide_type)
    correct_first = 1.0 - beta_first**step_float
    correct_second = 1.0 - beta_second**step_float
    renewed = []
    first_new = []
    second_new = []
    for group_id in range(6):
        clipped = grads[group_id] * clip_factor
        moment_one = beta_first * firsts[group_id] + (1.0 - beta_first) * clipped
        moment_two = beta_second * seconds[group_id] + (1.0 - beta_second) * clipped * clipped
        update = moment_one / correct_first / (jnp.sqrt(moment_two / correct_second) + adam_eps)
        if group_id < 4:
            update = update + decay_rate * masters[group_id]
        renewed.append(masters[group_id] - learn_rates[group_id] * update)
        first_new.append(moment_one)
        second_new.append(moment_two)
    layer_out = layer_rows.reshape(seqs_here, local_slots, model_width)
    grad_inputs = grad_in_rows.reshape(seqs_here, local_slots, model_width)
    return (
        (layer_out, grad_inputs, grad_norm) + tuple(renewed) + tuple(first_new) + tuple(second_new)
    )


def solution(mesh):
    token_spec = P("dp", "seq", None)
    matrix_spec = P(("dp", "seq"), None)
    row_spec = P(("dp", "seq"))
    group = (matrix_spec,) * 5 + (row_spec,)
    return jax.shard_map(
        per_device,
        mesh=mesh,
        in_specs=(token_spec, token_spec, P("dp"), P(), P(), P()) + group * 3,
        out_specs=(token_spec, token_spec, P()) + group * 3,
        check_vma=False,
    )
```

```python
import functools

import jax
import jax.numpy as jnp
from jax import lax
from jax.experimental import pallas as pl
from jax.experimental.pallas import tpu as pltpu
from jax.sharding import PartitionSpec as P

HEADS = 16
HD = 64
MESH = pl.DeviceIdType.MESH


norm_eps = 1e-05
neg_fill = -1e30
beta_first = 0.9
beta_second = 0.95
adam_eps = 1e-08
decay_rate = 0.1
clip_bound = 1.0


def flip(index, mask):
    return index + mask * (1 - 2 * ((index // mask) % 2))


class Place:
    def __init__(self, dp_size, seq_size):
        self.dp_size = dp_size
        self.depth = seq_size // 2
        self.bits = dp_size.bit_length() - 1
        self.dp = lax.axis_index("dp")
        seq = lax.axis_index("seq")
        self.z = seq // 2
        self.core = seq % 2
        self.masks = self.masks_of(self.core)

    def masks_of(self, core):
        return [
            (1 - core) * 2 ** (k % self.bits) + core * 2 ** ((k + 1) % self.bits)
            for k in range(self.bits)
        ]

    def leaving(self, core_masks=None):
        masks = self.masks if core_masks is None else core_masks
        order = []
        for k in range(self.bits - 1, -1, -1):
            order = order + self.span(flip(self.dp, masks[k]), k, masks)
        return order + [self.dp]

    def cube(self, k):
        return (flip(self.dp, self.masks[k]), self.z * 2 + self.core)

    def span(self, start, k, masks=None):
        found = [start]
        for mask in (self.masks if masks is None else masks)[:k]:
            found = found + [flip(one, mask) for one in found]
        return found

    def sibling(self):
        return (self.dp, self.z * 2 + 1 - self.core)

    def line(self, j):
        return (self.dp, ((self.z + j) % self.depth) * 2 + self.core)


def greet(peers):
    barrier = pltpu.get_barrier_semaphore()
    for peer in peers:
        pl.semaphore_signal(barrier, inc=1, device_id=peer, device_id_type=MESH)
    pl.semaphore_wait(barrier, len(peers))


class Gather:
    def __init__(self, at, sources, fulls, sems):
        self.at, self.sources, self.fulls = at, sources, fulls
        self.count = len(sources)
        self.local_sem, self.line_send, self.cube_send, self.pair_send, self.arrive = sems
        self.pending, self.local = [], []

    def send(self, a, source, row, level, peer, sem):
        core = self.at.core
        copy = pltpu.make_async_remote_copy(
            src_ref=source,
            dst_ref=self.fulls[a].at[row, level, core],
            send_sem=sem,
            recv_sem=self.arrive.at[a, row, level, core],
            device_id=peer,
            device_id_type=MESH,
        )
        copy.start()
        self.pending.append(copy)

    def received(self, a, row, level, side):
        block = self.fulls[a].at[row, level, side]
        pltpu.make_async_copy(block, block, self.arrive.at[a, row, level, side]).wait()

    def pass_on(self, a, source, row, slot, level, first):
        for k in range(first, self.at.bits):
            self.send(a, source, row, level, self.at.cube(k), self.cube_send.at[a, k, slot, level])
        self.send(a, source, row, level, self.at.sibling(), self.pair_send.at[a, slot, level])

    def start(self, a):
        at = self.at
        for j in range(1, at.depth):
            self.send(a, self.sources[a], at.dp, at.z, at.line(j), self.line_send.at[a, j - 1])
        self.pass_on(a, self.sources[a], at.dp, 0, at.z, 0)
        copy = pltpu.make_async_copy(
            self.sources[a], self.fulls[a].at[at.dp, at.z, at.core], self.local_sem.at[a]
        )
        copy.start()
        self.local.append(copy)

    def stage(self, a, stage):
        at = self.at
        if stage == 0:
            for j in range(at.depth - 1, 0, -1):
                level = (at.z + j) % at.depth
                self.received(a, at.dp, level, at.core)
                self.pass_on(a, self.fulls[a].at[at.dp, level, at.core], at.dp, 0, level, 0)
            return
        k = stage - 1
        for slot, row in enumerate(at.span(flip(at.dp, at.masks[k]), k)):
            for j in range(at.depth):
                level = (at.z + j) % at.depth
                self.received(a, row, level, at.core)
                block = self.fulls[a].at[row, level, at.core]
                self.pass_on(a, block, row, 2**k + slot, level, k + 1)

    def finish(self, a):
        for row in range(self.at.dp_size):
            for level in range(self.at.depth):
                self.received(a, row, level, 1 - self.at.core)
        self.local[a].wait()

    def drain(self):
        for copy in self.pending:
            copy.wait_send()


def gather_sems(count, dp_size, seq_size):
    depth, bits = seq_size // 2, dp_size.bit_length() - 1
    return [
        pltpu.SemaphoreType.DMA((count,)),
        pltpu.SemaphoreType.DMA((count, depth - 1)),
        pltpu.SemaphoreType.DMA((count, bits, dp_size, depth)),
        pltpu.SemaphoreType.DMA((count, dp_size, depth)),
        pltpu.SemaphoreType.DMA((count, dp_size, depth, 2)),
    ]


class Scatter:
    def __init__(self, at, sources, held, outs, buffers, sems):
        self.at, self.sources, self.held, self.outs = at, sources, held, outs
        count = self.count = len(sources)
        self.pair = buffers[:count]
        self.cube = [buffers[(1 + k) * count : (2 + k) * count] for k in range(at.bits)]
        self.line = buffers[(1 + at.bits) * count : (2 + at.bits) * count]
        (
            self.own_sem,
            self.pair_send,
            self.pair_recv,
            self.cube_send,
            self.cube_recv,
            self.line_send,
            self.line_recv,
        ) = sems
        self.pending = []
        self.order = at.leaving()
        self.theirs = at.leaving(at.masks_of(1 - at.core))
        self.all_hops = [(q, 0) for q in range(at.bits)]

    def fetch(self, a, spot):
        if self.held[a] is not None and spot < len(self.order):
            self.fetched(a, spot).start()

    def fetched(self, a, spot):
        row = self.order[spot]
        return pltpu.make_async_copy(
            self.sources[a].at[row, :, self.at.core],
            self.held[a].at[spot % 2],
            self.own_sem.at[a, spot],
        )

    def start(self, a):
        core = self.at.core
        self.fetch(a, 0)
        self.fetch(a, 1)
        for spot, other in enumerate(self.theirs):
            self.send(
                self.sources[a].at[other, :, 1 - core],
                self.pair[a].at[other],
                self.pair_send.at[a, spot],
                self.pair_recv.at[a, other],
                self.at.sibling(),
            )

    def ready(self, a, spot):
        row = self.order[spot]
        if self.held[a] is not None:
            self.fetched(a, spot).wait()
        block = self.pair[a].at[row]
        pltpu.make_async_copy(block, block, self.pair_recv.at[a, row]).wait()

    def landed(self, a, hops):
        for q, slot in hops:
            block = self.cube[q][a].at[slot]
            pltpu.make_async_copy(block, block, self.cube_recv.at[a, q, slot]).wait()

    def total(self, a, spot, level, rows, hops):
        row = self.order[spot]
        if self.held[a] is not None:
            value = self.held[a][spot % 2, level, rows].astype(jnp.float32)
        else:
            value = self.sources[a][row, level, self.at.core, rows].astype(jnp.float32)
        value = value + self.pair[a][row, level, rows].astype(jnp.float32)
        for k, slot in hops:
            value = value + self.cube[k][a][slot, level, rows].astype(jnp.float32)
        return value

    def each_chunk(self, a, body):
        height = self.pair[a].shape[2]
        step = min(16, height)
        if step == height:
            body(pl.ds(0, step))
        else:

            def one(i, carry):
                body(pl.ds(pl.multiple_of(i * step, step), step))
                return carry

            lax.fori_loop(0, height // step, one, 0)

    def fold(self, a, spot, level, hops):
        row = self.order[spot]

        def body(rows):
            value = self.total(a, spot, level, rows, hops)
            self.pair[a][row, level, rows] = value.astype(self.pair[a].dtype)

        self.each_chunk(a, body)

    def send(self, source, target, send_sem, recv_sem, peer):
        copy = pltpu.make_async_remote_copy(
            src_ref=source,
            dst_ref=target,
            send_sem=send_sem,
            recv_sem=recv_sem,
            device_id=peer,
            device_id_type=MESH,
        )
        copy.start()
        self.pending.append(copy)

    def cube_stage(self, a, k):
        at = self.at
        first = sum(2**q for q in range(k + 1, at.bits))
        for slot in range(2**k):
            spot = first + slot
            hops = [(q, 2**k + slot) for q in range(k + 1, at.bits)]
            self.ready(a, spot)
            self.landed(a, hops)

            def level_fold(level, carry, spot=spot, hops=hops):
                self.fold(a, spot, level, hops)
                return carry

            lax.fori_loop(0, at.depth, level_fold, 0)
            self.fetch(a, spot + 2)
            self.send(
                self.pair[a].at[self.order[spot]],
                self.cube[k][a].at[slot],
                self.cube_send.at[a, k, slot],
                self.cube_recv.at[a, k, slot],
                at.cube(k),
            )

    def line_stage(self, a):
        at = self.at
        spot = len(self.order) - 1
        self.ready(a, spot)
        self.landed(a, self.all_hops)
        for j in range(1, at.depth):
            level = (at.z + j) % at.depth
            self.fold(a, spot, level, self.all_hops)
            self.send(
                self.pair[a].at[at.dp, level],
                self.line[a].at[j - 1],
                self.line_send.at[a, j - 1],
                self.line_recv.at[a, j - 1],
                at.line(j),
            )

    def final_stage(self, a):
        at = self.at
        for j in range(1, at.depth):
            block = self.line[a].at[j - 1]
            pltpu.make_async_copy(block, block, self.line_recv.at[a, j - 1]).wait()
        out, first = self.outs[a]
        width = self.pair[a].shape[3]

        def body(rows):
            value = self.total(a, len(self.order) - 1, at.z, rows, self.all_hops)
            for j in range(1, at.depth):
                value = value + self.line[a][j - 1, rows].astype(jnp.float32)
            out[rows, first : first + width] = value

        self.each_chunk(a, body)

    def stage(self, a, stage):
        bits = self.at.bits
        if stage < bits:
            self.cube_stage(a, bits - 1 - stage)
        elif stage == bits:
            self.line_stage(a)
        else:
            self.final_stage(a)

    def drain(self):
        for copy in self.pending:
            copy.wait_send()


def skewed(count, stages):
    return [
        (step - stage, stage)
        for step in range(count + stages - 1)
        for stage in range(stages)
        if 0 <= step - stage < count
    ]


def scatter_buffers(tails, kinds, dp_size, seq_size):
    depth, bits = seq_size // 2, dp_size.bit_length() - 1
    found = []
    for lead in [(dp_size, depth)] + [(2**k, depth) for k in range(bits)] + [(depth - 1,)]:
        found += [pltpu.VMEM(lead + tail, kind) for tail, kind in zip(tails, kinds)]
    return found


def scatter_sems(count, dp_size, seq_size):
    depth, bits = seq_size // 2, dp_size.bit_length() - 1
    return [
        pltpu.SemaphoreType.DMA((count, dp_size)),
        pltpu.SemaphoreType.DMA((count, dp_size)),
        pltpu.SemaphoreType.DMA((count, dp_size)),
        pltpu.SemaphoreType.DMA((count, bits, dp_size // 2)),
        pltpu.SemaphoreType.DMA((count, bits, dp_size // 2)),
        pltpu.SemaphoreType.DMA((count, depth - 1)),
        pltpu.SemaphoreType.DMA((count, depth - 1)),
    ]


class Norm:
    def __init__(self, at, dp_size, seq_size, seq_part, dp_part, mine, send_sem, recv_sem):
        seq = at.z * 2 + at.core
        self.seq_peers = [(at.dp, (seq + j) % seq_size) for j in range(1, seq_size)]
        self.dp_peers = [((at.dp + j) % dp_size, seq) for j in range(1, dp_size)]
        self.seq_part, self.dp_part, self.mine = seq_part, dp_part, mine
        self.send_sem, self.recv_sem = send_sem, recv_sem

    def add_squares(self, ref, first, width):
        def one(i, carry):
            value = ref[pl.ds(pl.multiple_of(i * 8, 8), 8), first : first + width]
            squares = value * value
            part = squares[:, :128]
            for lane in range(1, width // 128):
                part = part + squares[:, lane * 128 : (lane + 1) * 128]
            self.mine[...] += part
            return carry

        lax.fori_loop(0, ref.shape[0] // 8, one, 0)

    def exchange(self, peers, parts, base):
        copies = []
        for i, peer in enumerate(peers):
            copy = pltpu.make_async_remote_copy(
                src_ref=self.mine,
                dst_ref=parts.at[i],
                send_sem=self.send_sem.at[base + i],
                recv_sem=self.recv_sem.at[base + i],
                device_id=peer,
                device_id_type=MESH,
            )
            copy.start()
            copies.append(copy)
        for copy in copies:
            copy.wait()
        value = self.mine[...]
        for i in range(len(peers)):
            value = value + parts[i]
        self.mine[...] = value

    def over_all(self):
        self.exchange(self.seq_peers, self.seq_part, 0)
        self.exchange(self.dp_peers, self.dp_part, len(self.seq_peers))
        return self.mine[...]


class Heads:
    def __init__(self, seq_size, pairs, seqs):
        self.seq_size, self.pairs = seq_size, pairs
        self.units = seqs * pairs // seq_size
        self.dp = lax.axis_index("dp")
        self.seq = lax.axis_index("seq")
        self.peers = [(self.seq + j) % seq_size for j in range(1, seq_size)]

    def share(self, seq, unit):
        return seq % self.pairs, (seq // self.pairs) * self.units + unit

    def start(self, copies):
        for copy in copies:
            copy.start()
        return copies

    def to_heads(self, rows, units, unit, sems):
        local_sem, send_sem, recv_sem = sems
        copies = []
        for j, peer in enumerate(self.peers):
            pair, which = self.share(peer, unit)
            copies.append(
                pltpu.make_async_remote_copy(
                    src_ref=rows.at[:, pair, which],
                    dst_ref=units.at[:, unit, self.seq],
                    send_sem=send_sem.at[0, unit, j],
                    recv_sem=recv_sem.at[0, unit, j],
                    device_id=(self.dp, peer),
                    device_id_type=MESH,
                )
            )
        pair, which = self.share(self.seq, unit)
        copies.append(
            pltpu.make_async_copy(
                rows.at[:, pair, which], units.at[:, unit, self.seq], local_sem.at[0, unit]
            )
        )
        return self.start(copies)

    def to_rows(self, units, rows, unit, sems):
        local_sem, send_sem, recv_sem = sems
        copies = []
        pair, which = self.share(self.seq, unit)
        for j, peer in enumerate(self.peers):
            copies.append(
                pltpu.make_async_remote_copy(
                    src_ref=units.at[:, unit, peer],
                    dst_ref=rows.at[:, pair, which],
                    send_sem=send_sem.at[1, unit, j],
                    recv_sem=recv_sem.at[1, unit, j],
                    device_id=(self.dp, peer),
                    device_id_type=MESH,
                )
            )
        copies.append(
            pltpu.make_async_copy(
                units.at[:, unit, self.seq], rows.at[:, pair, which], local_sem.at[1, unit]
            )
        )
        return self.start(copies)

    def unit_sequence(self, unit):
        return (self.seq // self.pairs) * self.units + unit


VMEM_SPEC = pl.BlockSpec(memory_space=pltpu.VMEM)


def head_lanes(rows, head):
    lane = lax.broadcasted_iota(jnp.int32, rows.shape, 1)
    return jnp.where(lane // HD == head, rows, jnp.zeros_like(rows))


CHUNK = 256


def attend(heads, unit, qkv, key_pos, query_pos, context, stats, pump):
    length = query_pos.shape[1]
    keys = qkv[1, unit].reshape(length, 128)
    values_t = qkv[2, unit].reshape(length, 128).T
    pos = key_pos[heads.unit_sequence(unit)][:, :1]

    def chunk(i, carry):
        where = pl.ds(pl.multiple_of(i * CHUNK, CHUNK), CHUNK)
        queries = context_rows(qkv.at[0, unit], where) * 0.125
        allowed = pos <= query_pos[:, where]
        halves = []
        for head in range(2):
            scores = contract_cols(keys, head_lanes(queries, head))
            scores = jnp.where(allowed, scores, neg_fill)
            top = jnp.max(scores, axis=0, keepdims=True)
            exp_scores = jnp.exp(scores - top)
            total = jnp.sum(exp_scores, axis=0, keepdims=True)
            weights = (exp_scores * (1.0 / total)).astype(jnp.bfloat16)
            stats[unit, head, :, where] = top + jnp.log(total)
            halves.append(
                jnp.dot(
                    values_t[head * HD : (head + 1) * HD],
                    weights,
                    preferred_element_type=jnp.float32,
                )
            )
        rows = jnp.concatenate(halves, axis=0).T.astype(jnp.bfloat16)
        store_rows(context.at[unit], where, rows)
        return carry

    in_pieces(length // CHUNK, chunk, pump)


def in_pieces(count, body, pump):
    pieces = min(count, max(1, len(pump)))
    for piece in range(pieces):
        lax.fori_loop(piece * count // pieces, (piece + 1) * count // pieces, body, 0)
        if pump:
            pump.pop(0)()


def context_rows(ref, where):
    slots = ref.shape[1]
    some = ref[pl.ds(where.start // slots, CHUNK // slots)]
    return some.reshape(CHUNK, 128)


def store_rows(ref, where, rows):
    slots = ref.shape[1]
    ref[pl.ds(where.start // slots, CHUNK // slots)] = rows.reshape(CHUNK // slots, slots, 128)


def attend_back(
    heads, unit, qkv, grad_ctx, key_pos, query_pos, stats, grads, key_sum, value_sum, pump
):
    length = query_pos.shape[1]
    keys = qkv[1, unit].reshape(length, 128)
    keys_t = keys.T
    values = qkv[2, unit].reshape(length, 128)
    pos = key_pos[heads.unit_sequence(unit)][:, :1]
    key_sum[...] = jnp.zeros_like(key_sum)
    value_sum[...] = jnp.zeros_like(value_sum)

    def chunk(i, carry):
        where = pl.ds(pl.multiple_of(i * CHUNK, CHUNK), CHUNK)
        queries = context_rows(qkv.at[0, unit], where) * 0.125
        grad_rows = context_rows(grad_ctx.at[unit], where)
        allowed = pos <= query_pos[:, where]
        halves = []
        for head in range(2):
            queries_h = head_lanes(queries, head)
            grad_h = head_lanes(grad_rows, head)
            scores = jnp.where(allowed, contract_cols(keys, queries_h), neg_fill)
            weights = jnp.exp(scores - stats[unit, head, :, where])
            grad_prob = contract_cols(values, grad_h)
            delta = jnp.sum(weights * grad_prob, axis=0, keepdims=True)
            grad_score = (weights * (grad_prob - delta)).astype(jnp.bfloat16)
            value_sum[...] += jnp.dot(
                weights.astype(jnp.bfloat16), grad_h, preferred_element_type=jnp.float32
            )
            key_sum[...] += jnp.dot(grad_score, queries_h, preferred_element_type=jnp.float32)
            halves.append(
                jnp.dot(
                    keys_t[head * HD : (head + 1) * HD],
                    grad_score,
                    preferred_element_type=jnp.float32,
                )
            )
        rows = (jnp.concatenate(halves, axis=0).T * 0.125).astype(jnp.bfloat16)
        store_rows(grads.at[0, unit], where, rows)
        return carry

    in_pieces(length // CHUNK, chunk, pump)
    shape = grads.shape[2:]
    grads[1, unit] = key_sum[...].astype(jnp.bfloat16).reshape(shape)
    grads[2, unit] = value_sum[...].astype(jnp.bfloat16).reshape(shape)


def exchange_sems(units, seq_size):
    return [
        pltpu.SemaphoreType.DMA((2, units)),
        pltpu.SemaphoreType.DMA((2, units, seq_size - 1)),
        pltpu.SemaphoreType.DMA((2, units, seq_size - 1)),
    ]


def head_columns(packed, model_width):
    devices = packed.shape[0]
    wide = model_width // devices
    spread = (
        lax.broadcasted_iota(jnp.int32, (128, model_width), 1) % wide
        == lax.broadcasted_iota(jnp.int32, (128, model_width), 0)
    )
    spread = spread.astype(jnp.float32).astype(jnp.bfloat16)
    tall = jnp.dot(packed.reshape(devices * 16, 128), spread, preferred_element_type=jnp.float32)
    tall = tall.reshape(devices, 16, model_width)
    device = lax.broadcasted_iota(jnp.int32, tall.shape, 0)
    lane = lax.broadcasted_iota(jnp.int32, tall.shape, 2)
    return jnp.sum(jnp.where(lane // wide == device, tall, 0.0), axis=0)


def front_kernel(dp_size, seq_size, count, tokens, *refs):
    sources, refs = refs[:count], refs[count:]
    (x_ref, key_pos, query_pos), refs = refs[:3], refs[3:]
    fulls, refs = list(refs[:count]), refs[count:]
    (context_out, qkv, stats), refs = refs[:3], refs[3:]
    (small_full, qkv_full, normed, rows, context), refs = refs[:5], refs[5:]
    out_sem, refs = refs[0], refs[1:]
    exchange, gather_sem = refs[:3], refs[3:]
    small_out, qkv_out = fulls[0], fulls[1]
    fulls[0], fulls[1] = small_full, qkv_full

    at = Place(dp_size, seq_size)
    pairs, seqs, slots = rows.shape[1:4]
    width = x_ref.shape[1]
    heads = Heads(seq_size, pairs, seqs)
    greet([(at.dp, peer) for peer in heads.peers] + [at.cube(k) for k in range(at.bits)])
    gather = Gather(at, sources, fulls, gather_sem)
    for a in range(count):
        gather.start(a)
    for stage in range(at.bits + 1):
        gather.stage(0, stage)
        gather.stage(1, stage)
    gather.finish(0)
    cols = head_columns(small_full[...].reshape(dp_size * seq_size, 16, 128), width)

    def norm_rows(i, carry):
        where = pl.ds(pl.multiple_of(i * 32, 32), 32)
        value = x_ref[where].astype(jnp.float32)
        normed[where] = layer_norm(value, cols[0:1], cols[1:2]).astype(jnp.bfloat16)
        return carry

    lax.fori_loop(0, x_ref.shape[0] // 32, norm_rows, 0)
    gather.finish(1)
    out_copies = [
        pltpu.make_async_copy(small_full, small_out, out_sem.at[0]),
        pltpu.make_async_copy(qkv_full, qkv_out, out_sem.at[1]),
    ]
    for copy in out_copies:
        copy.start()
    steps = width // 256
    for part in range(3):
        for step in range(steps):
            at_col = part * width + step * 256
            matrix = qkv_full[:, :, :, :, at_col : at_col + 256].reshape(width, 256)
            value = jnp.dot(normed[...], matrix, preferred_element_type=jnp.float32)
            if part != 1:
                row = 2 if part == 0 else 3
                value = value + cols[row : row + 1, step * 256 : (step + 1) * 256]
            value = value.astype(jnp.bfloat16)
            for half in range(2):
                rows[part, step * 2 + half] = value[:, half * 128 : (half + 1) * 128].reshape(
                    seqs, slots, 128
                )
    coming = [heads.to_heads(rows, qkv, unit, exchange) for unit in range(heads.units)]
    later = [(a + 2, stage) for a, stage in skewed(count - 2, at.bits + 1)]
    pump = [functools.partial(gather.stage, a, stage) for a, stage in later]
    for action in pump[: PUMP_FIRST]:
        action()
    pump = pump[PUMP_FIRST :]
    leaving = []
    for unit in range(heads.units):
        for copy in coming[unit]:
            copy.wait()
        attend(heads, unit, qkv, key_pos, query_pos, context.at[0], stats, pump)
        leaving = leaving + heads.to_rows(context, context_out, unit, exchange)
    for action in pump:
        action()
    for a in range(2, count):
        gather.finish(a)
    for copy in leaving + out_copies:
        copy.wait()
    gather.drain()


PUMP_FIRST = 4


def front(blocks, x_rows, key_pos, query_pos, seqs, dp_size, seq_size):
    count = len(blocks)
    tokens, width = x_rows.shape
    slots = tokens // seqs
    pairs = width // 128
    units = seqs * pairs // seq_size
    low = jnp.bfloat16
    lead = (dp_size, seq_size // 2, 2)
    shapes = [jax.ShapeDtypeStruct(lead + block.shape, block.dtype) for block in blocks]
    shapes += [
        jax.ShapeDtypeStruct((1, pairs, seqs, slots, 128), low),
        jax.ShapeDtypeStruct((3, units, seq_size, slots, 128), low),
        jax.ShapeDtypeStruct((units, 2, 1, seq_size * slots), jnp.float32),
    ]
    any_spec = pl.BlockSpec(memory_space=pl.ANY)
    return pl.pallas_call(
        functools.partial(front_kernel, dp_size, seq_size, count, tokens),
        out_shape=shapes,
        in_specs=[any_spec] * count + [VMEM_SPEC] * 3,
        out_specs=[any_spec] * count + [VMEM_SPEC] * 3,
        scratch_shapes=[
            pltpu.VMEM(lead + blocks[0].shape, low),
            pltpu.VMEM(lead + blocks[1].shape, low),
            pltpu.VMEM((tokens, width), low),
            pltpu.VMEM((3, pairs, seqs, slots, 128), low),
            pltpu.VMEM((1, units, seq_size, slots, 128), low),
            pltpu.SemaphoreType.DMA((2,)),
        ]
        + exchange_sems(units, seq_size)
        + gather_sems(count, dp_size, seq_size),
        compiler_params=pltpu.CompilerParams(
            collective_id=0, has_side_effects=True, vmem_limit_bytes=56 << 20
        ),
        name="front",
    )(*blocks, x_rows, key_pos, query_pos)


def device_rows(vec_rows, devices):
    count, model_width = vec_rows.shape
    wide = model_width // devices
    gather_lanes = (
        lax.broadcasted_iota(jnp.int32, (model_width, 128), 0) % wide
        == lax.broadcasted_iota(jnp.int32, (model_width, 128), 1)
    ).astype(jnp.float32)
    device = lax.broadcasted_iota(jnp.int32, (devices, model_width), 0)
    lane = lax.broadcasted_iota(jnp.int32, (devices, model_width), 1)
    place = lax.broadcasted_iota(jnp.int32, (devices, 16, 128), 1)
    value = jnp.zeros((devices, 16, 128), jnp.float32)
    for k in range(count):
        spread = jnp.where(lane // wide == device, vec_rows[k : k + 1], 0.0)
        part = jnp.dot(
            spread,
            gather_lanes,
            precision=lax.Precision.HIGHEST,
            preferred_element_type=jnp.float32,
        )
        value = value + jnp.where(place == k, part.reshape(devices, 1, 128), 0.0)
    return value


def back_kernel(dp_size, seq_size, count, *refs):
    at = Place(dp_size, seq_size)
    given, refs = refs[:count], refs[count:]
    (qkv_matrix, rows, qkv, stats, key_pos, query_pos), refs = refs[:6], refs[6:]
    (normed_t, x_ref, resid_ref, gain_ref, small_ref), refs = refs[:5], refs[5:]
    outs, refs = refs[: count + 2], refs[count + 2 :]
    (x_grad, norm_out), refs = refs[:2], refs[2:]
    held, refs = list(refs[:count]), refs[count:]
    total = count + 4
    buffers, refs = refs[: (2 + at.bits) * total], refs[(2 + at.bits) * total :]
    (parts, small, matrix, normed_grad, vec_rows), refs = refs[:5], refs[5:]
    (grad_ctx, unit_grads, key_sum, value_sum, grad_rows), refs = refs[:5], refs[5:]
    (seq_part, dp_part, mine, norm_send, norm_recv, matrix_sem), refs = refs[:6], refs[6:]
    exchange, scatter_sem = refs[:3], refs[3:]
    pairs, seqs, slots = rows.shape[1:4]
    tokens, width = x_ref.shape
    devices = dp_size * seq_size

    heads = Heads(seq_size, pairs, seqs)
    norm = Norm(at, dp_size, seq_size, seq_part, dp_part, mine, norm_send, norm_recv)
    greet(norm.seq_peers + norm.dp_peers)
    coming = [heads.to_heads(rows, grad_ctx, unit, exchange) for unit in range(heads.units)]
    sources = list(given) + [parts.at[part] for part in range(3)] + [small]
    targets = [(out, 0) for out in outs[:count]]
    targets += [(outs[count], part * width) for part in range(3)] + [(outs[count + 1], 0)]
    scatter = Scatter(at, sources, held + [None] * 4, targets, buffers, scatter_sem)
    for a in range(count):
        scatter.start(a)
    matrix_copies = [
        pltpu.make_async_copy(
            qkv_matrix.at[:, :, :, :, pl.ds(part * width, width)], matrix, matrix_sem.at[part]
        )
        for part in range(3)
    ]
    matrix_copies[0].start()
    mine[...] = jnp.zeros_like(mine)

    def run(a, stage):
        scatter.stage(a, stage)
        if stage == at.bits + 1:
            out, first = targets[a]
            norm.add_squares(out, first, scatter.pair[a].shape[3])

    early = [(a, 0) for a in range(count)]
    rest = [one for one in skewed(count, at.bits + 2) if one not in early]
    for one in early:
        run(*one)
    pump = [functools.partial(run, *one) for one in rest[:PUMP_BACK]]
    rest = rest[PUMP_BACK:]
    leaving = []
    for unit in range(heads.units):
        for copy in coming[unit]:
            copy.wait()
        attend_back(
            heads,
            unit,
            qkv,
            grad_ctx.at[0],
            key_pos,
            query_pos,
            stats,
            unit_grads,
            key_sum,
            value_sum,
            pump,
        )
        leaving = leaving + heads.to_rows(unit_grads, grad_rows, unit, exchange)
    for action in pump:
        action()
    for one in rest[:PUMP_MID]:
        run(*one)
    rest = rest[PUMP_MID:]
    for copy in leaving:
        copy.wait()

    high = width // dp_size
    for part in range(3):

        def one_tile(i, carry, part=part):
            pair = pl.ds(i * 2, 2)
            both = grad_rows[part, pair].reshape(2, tokens, 128)
            tile = jnp.concatenate([both[0], both[1]], axis=1)
            cols = pl.ds(pl.multiple_of(i * 256, 256), 256)
            if part != 1:
                row = 2 if part == 0 else 3
                vec_rows[row : row + 1, cols] = jnp.sum(
                    tile.astype(jnp.float32), axis=0, keepdims=True
                )
            for row in range(dp_size):
                value = jnp.dot(
                    normed_t[row * high : (row + 1) * high],
                    tile,
                    preferred_element_type=jnp.float32,
                )
                parts[part, row, :, :, :, cols] = value.astype(jnp.bfloat16).reshape(
                    parts.shape[2:5] + (256,)
                )
            return carry

        lax.fori_loop(0, width // 256, one_tile, 0)
        scatter.start(count + part)

    fresh = [(count + a, stage) for a, stage in skewed(3, at.bits + 2)]
    for one in fresh[:1]:
        run(*one)
    fresh = fresh[1:]

    normed_grad[...] = jnp.zeros_like(normed_grad)
    for part in range(3):
        matrix_copies[part].wait()

        def one_step(i, carry, part=part):
            cols = pl.ds(pl.multiple_of(i * 256, 256), 256)
            both = grad_rows[part, pl.ds(i * 2, 2)].reshape(2, tokens, 128)
            tile = jnp.concatenate([both[0], both[1]], axis=1)
            block = matrix[:, :, :, :, cols].reshape(width, 256)
            normed_grad[...] += contract_cols(tile, block)
            return carry

        lax.fori_loop(0, width // 256, one_step, 0)
        if part < 2:
            matrix_copies[part + 1].start()
        for one in (rest[:1] + fresh[:1]) if rest else fresh[:1]:
            run(*one)
        fresh = fresh[1:]
        rest = rest[1:]
    vec_rows[0:2] = jnp.zeros_like(vec_rows[0:2])

    def norm_rows(i, carry):
        where = pl.ds(pl.multiple_of(i * 32, 32), 32)
        value = x_ref[where].astype(jnp.float32)
        centered = value - jnp.mean(value, axis=-1, keepdims=True)
        variance = jnp.mean(centered * centered, axis=-1, keepdims=True)
        scale = lax.rsqrt(variance + norm_eps)
        unit_rows = centered * scale
        grad = normed_grad[where]
        vec_rows[0:1] += jnp.sum(grad * unit_rows, axis=0, keepdims=True)
        vec_rows[1:2] += jnp.sum(grad, axis=0, keepdims=True)
        grad = grad * gain_ref[...]
        first = jnp.mean(grad, axis=-1, keepdims=True)
        second = jnp.mean(grad * unit_rows, axis=-1, keepdims=True)
        x_grad[where] = resid_ref[where] + scale * (grad - first - unit_rows * second)
        return carry

    lax.fori_loop(0, tokens // 32, norm_rows, 0)
    mixed = small_ref[...] + device_rows(vec_rows[0:4], devices).reshape(small_ref.shape)
    small[...] = mixed
    scatter.start(count + 3)
    last = [(count + 3, stage) for stage in range(at.bits + 2)]
    for one in rest:
        run(*one)
    while fresh or last:
        for one in fresh[:2] + last[:1]:
            run(*one)
        fresh, last = fresh[2:], last[1:]
    norm_out[...] = norm.over_all()
    scatter.drain()


PUMP_BACK = 0
PUMP_MID = 5


def back(
    grads,
    qkv_matrix,
    rows,
    qkv,
    stats,
    key_pos,
    query_pos,
    normed_t,
    x_rows,
    resid_grad,
    gain,
    small,
    dp_size,
    seq_size,
):
    count = len(grads)
    pairs, seqs, slots = rows.shape[1:4]
    tokens, width = x_rows.shape
    units = seqs * pairs // seq_size
    length = seq_size * slots
    depth = seq_size // 2
    low, wide = jnp.bfloat16, jnp.float32
    lead = (dp_size, depth, 2)
    high = qkv_matrix.shape[3]
    tails = [grad.shape[3:] for grad in grads]
    all_tails = tails + [(high, width)] * 3 + [small.shape[3:]]
    kinds = [low] * (count + 3) + [wide]
    shapes = [
        jax.ShapeDtypeStruct(tail, wide) for tail in tails + [(high, 3 * width), small.shape[3:]]
    ]
    shapes += [
        jax.ShapeDtypeStruct((tokens, width), wide),
        jax.ShapeDtypeStruct((8, 128), wide),
    ]
    any_spec = pl.BlockSpec(memory_space=pl.ANY)
    return pl.pallas_call(
        functools.partial(back_kernel, dp_size, seq_size, count),
        out_shape=shapes,
        in_specs=[any_spec] * (count + 1) + [VMEM_SPEC] * 10,
        out_specs=[VMEM_SPEC] * (count + 4),
        scratch_shapes=[pltpu.VMEM((2, depth) + tail, low) for tail in tails]
        + scatter_buffers(all_tails, kinds, dp_size, seq_size)
        + [
            pltpu.VMEM((3,) + lead + (high, width), low),
            pltpu.VMEM(small.shape, wide),
            pltpu.VMEM(lead + (high, width), low),
            pltpu.VMEM((tokens, width), wide),
            pltpu.VMEM((8, width), wide),
            pltpu.VMEM((1, units, seq_size, slots, 128), low),
            pltpu.VMEM((3, units, seq_size, slots, 128), low),
            pltpu.VMEM((length, 128), wide),
            pltpu.VMEM((length, 128), wide),
            pltpu.VMEM((3,) + rows.shape[1:], low),
            pltpu.VMEM((seq_size - 1, 8, 128), wide),
            pltpu.VMEM((dp_size - 1, 8, 128), wide),
            pltpu.VMEM((8, 128), wide),
            pltpu.SemaphoreType.DMA((seq_size + dp_size - 2,)),
            pltpu.SemaphoreType.DMA((seq_size + dp_size - 2,)),
            pltpu.SemaphoreType.DMA((3,)),
        ]
        + exchange_sems(units, seq_size)
        + scatter_sems(count + 4, dp_size, seq_size),
        compiler_params=pltpu.CompilerParams(
            collective_id=2, has_side_effects=True, vmem_limit_bytes=60 << 20
        ),
        name="back",
    )(
        *grads,
        qkv_matrix,
        rows,
        qkv,
        stats,
        key_pos,
        query_pos,
        normed_t,
        x_rows,
        resid_grad,
        gain,
        small,
    )


def contract_rows(left, right):
    return lax.dot_general(
        left, right, (((0,), (0,)), ((), ())), preferred_element_type=jnp.float32
    )


def contract_cols(left, right):
    return lax.dot_general(
        left, right, (((1,), (1,)), ((), ())), preferred_element_type=jnp.float32
    )


def layer_norm(values, gain_vec, shift_vec):
    centered = values - jnp.mean(values, axis=-1, keepdims=True)
    variance = jnp.mean(centered * centered, axis=-1, keepdims=True)
    return centered * lax.rsqrt(variance + norm_eps) * gain_vec + shift_vec


def slot_positions(slot_ids, order_table, block_len):
    block_ids = jnp.arange(order_table.shape[0], dtype=jnp.int32)
    one_hot = (slot_ids[:, None] // block_len == block_ids[None, :]).astype(jnp.int32)
    picked = jnp.sum(one_hot * order_table[None, :], axis=1)
    return picked * block_len + slot_ids % block_len


def pack_small(vec_cols, bias, devices):
    wide = vec_cols.shape[1] // devices
    parts = vec_cols.reshape(8, devices, wide).transpose(1, 0, 2)
    parts = jnp.pad(parts, ((0, 0), (0, 0), (0, 128 - wide)))
    high = bias.shape[0] // devices
    last = jnp.pad(bias.reshape(devices, 1, high), ((0, 0), (0, 7), (0, 128 - high)))
    return jnp.concatenate([parts, last], axis=1)


def unpack_small(packed, model_width, hidden):
    devices = packed.shape[0]
    wide, high = model_width // devices, hidden // devices
    cols = packed[:, :8, :wide].transpose(1, 0, 2).reshape(8, model_width)
    return cols, packed[:, 8, :high].reshape(hidden)


def per_device(
    inputs,
    cotangent,
    lengths,
    block_order,
    step_count,
    learn_rates,
    w_qkv,
    w_proj,
    w_expand,
    w_shrink,
    vectors,
    bias_expand,
    first_qkv,
    first_proj,
    first_expand,
    first_shrink,
    first_vectors,
    first_bias,
    second_qkv,
    second_proj,
    second_expand,
    second_shrink,
    second_vectors,
    second_bias,
):
    low_type = jnp.bfloat16
    wide_type = jnp.float32
    dp_size, seq_size = lax.axis_size("dp"), lax.axis_size("seq")
    devices = dp_size * seq_size
    lead = (dp_size, seq_size // 2, 2)
    seqs_here, local_slots, model_width = inputs.shape
    hidden = w_expand.shape[1]
    total_slots = local_slots * seq_size
    block_len = total_slots // block_order.shape[0]
    token_count = seqs_here * local_slots
    first_slot = lax.axis_index("seq") * local_slots
    local_pos = slot_positions(
        first_slot + jnp.arange(local_slots, dtype=jnp.int32), block_order, block_len
    )
    key_pos = slot_positions(jnp.arange(total_slots, dtype=jnp.int32), block_order, block_len)
    valid_rows = (local_pos[None, :] < lengths[:, None]).astype(wide_type)
    rows_in = inputs.reshape(token_count, model_width).astype(wide_type)

    pairs = model_width // 128
    row_shape = (seqs_here, local_slots, -1, pairs, 128)
    far = jnp.where(key_pos[None, :] < lengths[:, None], key_pos[None, :], 2**30)
    key_limits = jnp.broadcast_to(far[:, :, None], (seqs_here, total_slots, 128))
    query_row = key_pos[None, :]
    small_block = pack_small(vectors.T, bias_expand, 1)[0].astype(low_type)
    gathered = front(
        [
            small_block,
            w_qkv.astype(low_type),
            w_proj.astype(low_type),
            w_expand.astype(low_type),
            w_shrink.astype(low_type),
        ],
        inputs.reshape(token_count, model_width),
        key_limits,
        query_row,
        seqs_here,
        dp_size,
        seq_size,
    )
    proj_full = gathered[2].reshape(model_width, -1)
    expand_full = gathered[3].reshape(model_width, -1)
    shrink_full = gathered[4].reshape(hidden, -1)
    context, qkv_units, row_stats = gathered[5:]
    vec_cols, bias_full = unpack_small(
        gathered[0].reshape(devices, 16, 128).astype(wide_type), model_width, hidden
    )
    gain_one, shift_one, _, _, bias_proj, gain_two, shift_two, bias_shrink = [
        vec_cols[i] for i in range(8)
    ]
    normed_one = layer_norm(rows_in, gain_one, shift_one).astype(low_type)
    context_low = context[0].transpose(1, 2, 0, 3).reshape(token_count, model_width)
    attn_rows = jnp.dot(context_low, proj_full, preferred_element_type=wide_type) + bias_proj
    resid = rows_in + attn_rows
    normed_two = layer_norm(resid, gain_two, shift_two).astype(low_type)
    pre_act = jnp.dot(normed_two, expand_full, preferred_element_type=wide_type) + bias_full
    gelu_out, gelu_back = jax.vjp(lambda arg_in: jax.nn.gelu(arg_in, approximate=True), pre_act)
    act_low = gelu_out.astype(low_type)
    layer_rows = (
        resid + jnp.dot(act_low, shrink_full, preferred_element_type=wide_type) + bias_shrink
    )
    grad_rows = (cotangent.astype(wide_type) * valid_rows[:, :, None]).reshape(
        token_count, model_width
    )
    grad_low = grad_rows.astype(low_type)
    grad_shrink = contract_rows(act_low, grad_low)
    grad_bias_shrink = jnp.sum(grad_rows, axis=0)
    grad_act = contract_cols(grad_low, shrink_full)
    grad_pre = gelu_back(grad_act)[0].astype(low_type)
    grad_expand = contract_rows(normed_two, grad_pre)
    grad_bias_expand = jnp.sum(grad_pre, axis=0, dtype=wide_type)
    grad_normed_two = contract_cols(grad_pre, expand_full)
    norm_two_out, norm_back_two = jax.vjp(layer_norm, resid, gain_two, shift_two)
    grad_resid_part, grad_gain_two, grad_shift_two = norm_back_two(grad_normed_two)
    grad_resid = grad_rows + grad_resid_part
    grad_attn_low = grad_resid.astype(low_type)
    grad_proj = contract_rows(context_low, grad_attn_low)
    grad_bias_proj = jnp.sum(grad_attn_low, axis=0, dtype=wide_type)
    grad_context = contract_cols(grad_attn_low, proj_full).astype(low_type)
    grad_context = grad_context.reshape(row_shape).transpose(2, 3, 0, 1, 4)
    nothing = jnp.zeros_like(gain_one)
    grad_cols = jnp.stack(
        [
            nothing,
            nothing,
            nothing,
            nothing,
            grad_bias_proj,
            grad_gain_two,
            grad_shift_two,
            grad_bias_shrink,
        ],
        axis=0,
    )
    small_grad = pack_small(grad_cols, grad_bias_expand, devices)
    (
        grad_shrink_mine,
        grad_expand_mine,
        grad_proj_mine,
        grad_qkv_mine,
        small_mine,
        grad_in_rows,
        squares,
    ) = back(
        [
            grad_shrink.astype(low_type).reshape(lead + w_shrink.shape),
            grad_expand.astype(low_type).reshape(lead + w_expand.shape),
            grad_proj.astype(low_type).reshape(lead + w_proj.shape),
        ],
        gathered[1],
        grad_context,
        qkv_units,
        row_stats,
        key_limits,
        query_row,
        normed_one.T,
        inputs.reshape(token_count, model_width),
        grad_resid,
        gain_one[None, :],
        small_grad.reshape(lead + small_grad.shape[1:]),
        dp_size,
        seq_size,
    )
    vec_mine, grad_bias_mine = unpack_small(
        small_mine[None], model_width // devices, hidden // devices
    )
    grad_vec_mine = vec_mine.T
    grads = (
        grad_qkv_mine,
        grad_proj_mine,
        grad_expand_mine,
        grad_shrink_mine,
        grad_vec_mine,
        grad_bias_mine,
    )
    masters = (w_qkv, w_proj, w_expand, w_shrink, vectors, bias_expand)
    firsts = (first_qkv, first_proj, first_expand, first_shrink, first_vectors, first_bias)
    seconds = (second_qkv, second_proj, second_expand, second_shrink, second_vectors, second_bias)
    grad_norm = jnp.sqrt(jnp.sum(squares))
    clip_factor = clip_bound / jnp.maximum(grad_norm, clip_bound)
    step_float = step_count.astype(wide_type)
    correct_first = 1.0 - beta_first**step_float
    correct_second = 1.0 - beta_second**step_float
    renewed = []
    first_new = []
    second_new = []
    for group_id in range(6):
        clipped = grads[group_id] * clip_factor
        moment_one = beta_first * firsts[group_id] + (1.0 - beta_first) * clipped
        moment_two = beta_second * seconds[group_id] + (1.0 - beta_second) * clipped * clipped
        update = moment_one / correct_first / (jnp.sqrt(moment_two / correct_second) + adam_eps)
        if group_id < 4:
            update = update + decay_rate * masters[group_id]
        renewed.append(masters[group_id] - learn_rates[group_id] * update)
        first_new.append(moment_one)
        second_new.append(moment_two)
    layer_out = layer_rows.reshape(seqs_here, local_slots, model_width)
    grad_inputs = grad_in_rows.reshape(seqs_here, local_slots, model_width)
    return (
        (layer_out, grad_inputs, grad_norm) + tuple(renewed) + tuple(first_new) + tuple(second_new)
    )


def solution(mesh):
    token_spec = P("dp", "seq", None)
    matrix_spec = P(("dp", "seq"), None)
    row_spec = P(("dp", "seq"))
    group = (matrix_spec,) * 5 + (row_spec,)
    return jax.shard_map(
        per_device,
        mesh=mesh,
        in_specs=(token_spec, token_spec, P("dp"), P(), P(), P()) + group * 3,
        out_specs=(token_spec, token_spec, P()) + group * 3,
        check_vma=False,
    )
```
